1024 devices in a mesh: section: 32 (over x, z_hi, y), tp: 32 (over z_lo, core).
Axes of the slice: x: 4, y: 4, z: 32 (z_hi: 2, z_lo: 16; z = z_hi * 16 + z_lo), core: 2. Of those that a mesh axis runs over, the one named last changes fastest.
Arguments:
- head_outputs: bfloat16 [32, 128, 8192], P('section', None, 'tp'), may hold values from -6 to 6
- residual: bfloat16 [32, 128, 8192], P('section', 'tp'), may hold values from -38 to 38
- out_weight: bfloat16 [8192, 8192], P('tp'), may hold values from -0.0625 to 0.0625
- norm_gain: bfloat16 [8192], replicated, may hold values from 0.099609375 to 1.8984375
- prior_peak: float32 [32], P('section'), may hold values from 6 to 48
- qkv_weight: bfloat16 [8192, 9216], P(None, 'tp'), may hold values from -0.0625 to 0.0625
Outputs:
- stream: bfloat16 [32, 128, 8192], P('section', 'tp')
- projected: bfloat16 [32, 128, 9216], P('section', None, 'tp')
- group_peak: float32 [32], P('section')
The draws below stay inside these ranges and needn't reach their ends.
All inputs are finite; a program needn't handle non-finite values.
Results may differ from the reference program's by a relative error of at most 0.02.
Values may be sent and summed in bfloat16 or wider, within the bound.
No kernel may reach another device: no remote copies, remote signals or barrier semaphores. Data moves between devices by JAX's collectives and lax.ppermute only.
A program may use at most 64 MiB of HBM per device.

```python
import math
import jax
import jax.numpy as jnp
from jax import lax

D = 8192
HQ = 64
HD = 128
TOK = 128
SECTIONS = 32
QKV = 9216
N_TP = 32


def draw_residual(key, part):
    first_key, second_key = jax.random.split(jax.random.fold_in(key, 11))
    bulk = jax.random.truncated_normal(first_key, -6.0, 6.0, (SECTIONS, TOK, D), jnp.float32)
    channel = jax.random.randint(second_key, (SECTIONS, TOK, 1), 0, D)
    position = jnp.arange(TOK).astype(jnp.float32) / max(TOK - 1, 1)
    amplitude = 8.0 * jnp.power(4.0, position)
    onehot = (jnp.arange(D)[None, None, :] == channel).astype(jnp.float32)
    return (bulk + onehot * amplitude[None, :, None]).astype(jnp.bfloat16)


def raised(array, rng, source, target, parts, factor):
    owner, partner = [(jnp.arange(array.shape[dim]) // (array.shape[dim] // parts)).reshape([-1 if axis == dim else 1 for axis in range(array.ndim)]) for dim in (source, target)]
    chosen = jax.random.permutation(rng, parts)[partner]
    strong = (owner == chosen) | (owner == (partner + parts // 2) % parts)
    return jnp.where(strong, factor * array, array)


def levels(own_key, dims, cuts, least, high):
    level, own = 1.0, jax.random.fold_in(own_key, 6)
    for axis_at, parts in cuts:
        steps = jnp.exp(jax.random.uniform(jax.random.fold_in(own, axis_at), (parts,), jnp.float32, least / len(cuts), high / len(cuts)))
        level = level * jnp.repeat(steps, dims[axis_at] // parts).reshape([-1 if axis == axis_at else 1 for axis in range(len(dims))])
    return level


def noise(rng, shape, width, limit, pieces=(), kind=jnp.bfloat16):
    entries = jax.random.normal(rng, shape, jnp.float32) * width
    if len(pieces) > 0:
        entries = levels(rng, shape, pieces, -0.22, 0.18) * entries
    return jnp.clip(entries, min=-limit, max=limit).astype(kind)


def noise_with(rng, extent, deviation, limit, cuts, heavy, held_as=jnp.bfloat16):
    array = deviation * jax.random.normal(rng, extent, jnp.float32)
    if cuts:
        array = array * levels(rng, extent, cuts, -0.22, 0.18)
    return jnp.clip(raised(array, jax.random.fold_in(rng, 3), *heavy), -limit, limit).astype(held_as)


def setup_inputs(seed: int = 0) -> dict:
    key_list = jax.random.split(jax.random.key(seed), 7)
    return {
        "head_outputs": noise_with(key_list[0], (SECTIONS, TOK, HQ * HD), 1.0, 6.0, ((0, 32), (2, 32)), (2, 1, 32, 2.75)),
        "residual": draw_residual(jax.random.fold_in(key_list[6], 71), 0),
        "out_weight": noise(key_list[2], (HQ * HD, D), (HQ * HD) ** -0.5, 0.0625, ((0, 32),)),
        "norm_gain": jnp.clip(1.0 + 0.18 * jax.random.normal(key_list[3], (D,), jnp.float32), 0.099609375, 1.8984375).astype(jnp.bfloat16),
        "prior_peak": jnp.clip(jnp.exp(math.log(48.0) - 2.0794415 * jax.random.uniform(key_list[4], (SECTIONS,), jnp.float32) ** levels(key_list[4], (SECTIONS,), ((0, 32),), -0.2, 0.2)), 6.0, 48.0),
        "qkv_weight": noise(key_list[5], (D, QKV), D ** -0.5, 0.0625, ((1, 32),)),
    }


epsilon = 1e-05
ceiling = 448.0

def normalize(stream_rows, norm_gain):
    widened = stream_rows.astype(jnp.float32)
    mean_square = lax.optimization_barrier(jnp.mean(widened * widened, axis=-1, keepdims=True))
    return widened * lax.rsqrt(mean_square + epsilon) * norm_gain.astype(jnp.float32)

def reference(head_outputs, residual, out_weight, norm_gain, prior_peak, qkv_weight):
    head_width = HQ * HD // N_TP
    blocks = out_weight.reshape(N_TP, head_width, D)

    def section_forward(inputs):
        heads_section, resid_section, peak_section = inputs
        split_heads = heads_section.reshape(TOK, N_TP, head_width).transpose(1, 0, 2)

        def accumulate(running, paired):
            portion, weight_block = paired
            partial_value = jnp.dot(portion, weight_block, preferred_element_type=jnp.float32)
            rounded = lax.optimization_barrier(partial_value.astype(jnp.bfloat16))
            return (running + rounded.astype(jnp.float32), None)
        summed, unused = lax.scan(accumulate, jnp.zeros((TOK, D), jnp.float32), (split_heads, blocks))
        stream = (resid_section.astype(jnp.float32) + summed).astype(jnp.bfloat16)
        normed = normalize(stream, norm_gain)
        scale_unit = (peak_section / ceiling).astype(jnp.bfloat16)
        quantized = jnp.clip(normed / scale_unit.astype(jnp.float32), -ceiling, ceiling).astype(jnp.bfloat16)
        peak_value = jnp.max(jnp.abs(normed))
        return (stream, quantized, scale_unit, peak_value)
    stream, quantized, scale_unit, peak_value = lax.map(section_forward, (head_outputs, residual, prior_peak))
    arrived = jnp.roll(quantized, 1, axis=0)
    arrived_unit = jnp.roll(scale_unit, 1, axis=0)

    def project(inputs):
        arrived_rows, unit_in = inputs
        product = jnp.dot(arrived_rows, qkv_weight, preferred_element_type=jnp.float32)
        return (product * unit_in.astype(jnp.float32)).astype(jnp.bfloat16)
    projected = lax.map(project, (arrived, arrived_unit))
    return (stream, projected, peak_value)
```

```python
import functools
import jax
import jax.numpy as jnp
from jax import lax
from jax.experimental import pallas as pl
from jax.experimental.pallas import tpu as pltpu
from jax.sharding import PartitionSpec as P

epsilon = 1e-05
ceiling = 448.0

TP = 32
CHIPS = 16
ROWS = 8
TOK = 128
D = 8192
HALF = 4096
TAIL = 128
f32 = jnp.float32
bf16 = jnp.bfloat16


def across(x, d):
    return lax.ppermute(x, "tp", [(i, i ^ (2 * d)) for i in range(TP)])


def other_core(x):
    return lax.ppermute(x, "tp", [(i, i ^ 1) for i in range(TP)])


def next_section(x, sections):
    pairs = []
    for s in range(sections):
        shift = 16 if s % 4 == 3 else 0
        for t in range(TP):
            pairs.append((s * TP + t, ((s + 1) % sections) * TP + (t ^ shift)))
    return lax.ppermute(x, ("section", "tp"), pairs)


def shuffle(z):
    row = lax.broadcasted_iota(jnp.int32, (TOK, TOK), 0)
    col = lax.broadcasted_iota(jnp.int32, (TOK, TOK), 1)
    want = (((row // ROWS) ^ z) * ROWS) + row % ROWS
    return jnp.where(want == col, 1.0, 0.0).astype(bf16)


N_TILE = 1024


def out_proj_body(ids, heads, weight, resid, out, rows):
    z = ids[0]
    core = ids[1]

    @pl.when(pl.program_id(0) == 0)
    def _():
        rows[...] = jnp.dot(shuffle(z), heads[...], preferred_element_type=f32).astype(bf16)

    product = jnp.dot(rows[...], weight[...], preferred_element_type=f32)
    out[...] = product.astype(out.dtype)
    mine = resid[...].astype(f32)
    zero = jnp.zeros_like(mine)
    eight = jnp.where(core == 0, jnp.concatenate([mine, zero], 0), jnp.concatenate([zero, mine], 0))
    out[0:ROWS, :] = (product[0:ROWS, :] + eight).astype(out.dtype)


def out_proj(ids, heads, weight, resid, dtype):
    tiles = HALF // N_TILE
    return pl.pallas_call(
        out_proj_body,
        out_shape=jax.ShapeDtypeStruct((TOK, HALF), dtype),
        grid_spec=pltpu.PrefetchScalarGridSpec(
            num_scalar_prefetch=1,
            grid=(tiles,),
            in_specs=[
                pl.BlockSpec((TOK, 256), lambda i, ids: (0, 0)),
                pl.BlockSpec((256, N_TILE), lambda i, ids: (0, ids[2] * tiles + i)),
                pl.BlockSpec((4, N_TILE), lambda i, ids: (0, ids[2] * tiles + i)),
            ],
            out_specs=pl.BlockSpec((TOK, N_TILE), lambda i, ids: (0, i)),
            scratch_shapes=[pltpu.VMEM((TOK, 256), bf16)],
        ),
        name="out_proj",
    )(ids, heads, weight, resid)


K_TILE = 1024


def first_half_body(ids, a, weight, out):
    part = jnp.dot(a[...], weight[...], preferred_element_type=f32)

    @pl.when(pl.program_id(0) == 0)
    def _():
        out[...] = part

    @pl.when(pl.program_id(0) > 0)
    def _():
        out[...] += part


def first_half(ids, a, weight):
    steps = HALF // K_TILE
    n = weight.shape[1]
    return pl.pallas_call(
        first_half_body,
        out_shape=jax.ShapeDtypeStruct((TOK, n), f32),
        grid_spec=pltpu.PrefetchScalarGridSpec(
            num_scalar_prefetch=1,
            grid=(steps,),
            in_specs=[
                pl.BlockSpec((TOK, K_TILE), lambda i, ids: (0, i)),
                pl.BlockSpec((K_TILE, n), lambda i, ids: (ids[2] * steps + i, 0)),
            ],
            out_specs=pl.BlockSpec((TOK, n), lambda i, ids: (0, 0)),
        ),
        name="first_half",
    )(ids, a, weight)


def second_half_body(ids, a, weight, start, unit, out, acc):
    i = pl.program_id(0)
    part = jnp.dot(a[...], weight[...], preferred_element_type=f32)

    @pl.when(i == 0)
    def _():
        acc[...] = start[...] + part

    @pl.when(i > 0)
    def _():
        acc[...] += part

    @pl.when(i == pl.num_programs(0) - 1)
    def _():
        scaled = (acc[...] * unit[0, 0]).astype(bf16)
        out[...] = jnp.dot(shuffle(ids[0]), scaled, preferred_element_type=f32).astype(bf16)


def second_half(ids, a, weight, start, unit):
    steps = HALF // K_TILE
    n = weight.shape[1]
    return pl.pallas_call(
        second_half_body,
        out_shape=jax.ShapeDtypeStruct((TOK, n), bf16),
        grid_spec=pltpu.PrefetchScalarGridSpec(
            num_scalar_prefetch=1,
            grid=(steps,),
            in_specs=[
                pl.BlockSpec((TOK, K_TILE), lambda i, ids: (0, i)),
                pl.BlockSpec((K_TILE, n), lambda i, ids: (ids[2] * steps + i, 0)),
                pl.BlockSpec((TOK, n), lambda i, ids: (0, 0)),
                pl.BlockSpec(memory_space=pltpu.SMEM),
            ],
            out_specs=pl.BlockSpec((TOK, n), lambda i, ids: (0, 0)),
            scratch_shapes=[pltpu.VMEM((TOK, n), f32)],
        ),
        name="second_half",
    )(ids, a, weight, start, unit)


def cat(*blocks):
    return jnp.concatenate(blocks, axis=0)


def split(x):
    return [x[k * ROWS : (k + 1) * ROWS] for k in range(x.shape[0] // ROWS)]


def reduce_rounds(p):
    def send(d, *which):
        got = across(cat(*[p[o].astype(bf16) for o in which]), d)
        return [g.astype(f32) for g in split(got)]

    (a,) = send(1, 15)
    p[14] = p[14] + a
    b13, b11, b7 = send(1, 13, 11, 7)
    (b14,) = send(2, 14)
    p[12] = p[12] + b13 + b14
    p[10] = p[10] + b11
    p[6] = p[6] + b7
    c9, c5, c3 = send(1, 9, 5, 3)
    c10, c6 = send(2, 10, 6)
    (c12,) = send(4, 12)
    p[8] = p[8] + c9 + c10 + c12
    p[4] = p[4] + c5 + c6
    p[2] = p[2] + c3
    (d8,) = send(8, 8)
    (d4,) = send(4, 4)
    (d2,) = send(2, 2)
    (d1,) = send(1, 1)
    return p[0] + d1 + d2 + d4 + d8


def gather_rounds(own):
    b = {0: own}
    for d in (1, 2, 4, 8):
        b[d] = across(own, d)
    b[9], b[5], b[3] = split(across(cat(b[8], b[4], b[2]), 1))
    b[10], b[6] = split(across(cat(b[8], b[4]), 2))
    b[12] = across(b[8], 4)
    b[14] = across(b[12], 2)
    b[13], b[11], b[7] = split(across(cat(b[12], b[10], b[6]), 1))
    b[15] = across(b[14], 1)
    return cat(*[b[o] for o in range(CHIPS)])


def shards(sections, head_outputs, residual, out_weight, norm_gain, prior_peak, qkv_weight):
    heads = head_outputs[0]
    resid = residual[0]
    section = lax.axis_index("section")
    place = lax.axis_index("tp")
    z = place // 2
    core = place % 2
    scale_unit = (prior_peak / ceiling).astype(bf16)

    ids_own = jnp.stack([z, core, core]).astype(jnp.int32)
    ids_other = jnp.stack([z, core, 1 - core]).astype(jnp.int32)
    outgoing = out_proj(ids_other, heads, out_weight, resid, bf16)
    incoming = other_core(outgoing)
    kept = out_proj(ids_own, heads, out_weight, resid, f32)
    p = [k + i.astype(f32) for k, i in zip(split(kept), split(incoming))]
    own = lax.reduce_precision(reduce_rounds(p), 8, 7).astype(bf16)
    twin = other_core(own)

    wide = own.astype(f32)
    wide_twin = twin.astype(f32)
    total = jnp.sum(wide * wide, axis=-1, keepdims=True) + jnp.sum(wide_twin * wide_twin, axis=-1, keepdims=True)
    gain = lax.dynamic_slice_in_dim(norm_gain, core * HALF, HALF, 0).astype(f32)
    normed = wide * lax.rsqrt(total / D + epsilon) * gain
    quantized = jnp.clip(normed / scale_unit.astype(f32), -ceiling, ceiling).astype(bf16)
    tail = jnp.broadcast_to(scale_unit.reshape(1, 1), (ROWS, TAIL))
    arrived = next_section(jnp.concatenate([quantized, tail], axis=1), sections)

    peak = jnp.max(jnp.abs(normed))
    high = lax.reduce_precision(peak, 8, 7)
    low = (peak - high).astype(bf16)
    high = high.astype(bf16)
    lane = lax.broadcasted_iota(jnp.int32, (ROWS, TAIL), 1)
    peaks = jnp.where(lane == 0, high, low)
    payload = jnp.concatenate([arrived[:, :HALF], peaks], axis=1)
    unit = arrived[0:1, HALF : HALF + 1].astype(f32)
    mine = gather_rounds(payload)
    theirs = other_core(mine)

    label = z ^ jnp.where(section % 4 == 0, 8, 0)
    ids_first = jnp.stack([label, core, core]).astype(jnp.int32)
    ids_second = jnp.stack([label, core, 1 - core]).astype(jnp.int32)
    started = first_half(ids_first, mine, qkv_weight)
    projected = second_half(ids_second, theirs, qkv_weight, started, unit)

    tails = jnp.concatenate([mine[:, HALF : HALF + 2], theirs[:, HALF : HALF + 2]], axis=0).astype(f32)
    group_peak = jnp.max(tails[:, 0] + tails[:, 1]).reshape(1)

    first_row = (core == 0)
    own_rows = jnp.where(first_row, own[0:4], own[4:8])
    twin_rows = jnp.where(first_row, twin[0:4], twin[4:8])
    stream = jnp.where(
        first_row,
        jnp.concatenate([own_rows, twin_rows], axis=1),
        jnp.concatenate([twin_rows, own_rows], axis=1),
    )
    return (stream[None], projected[None], group_peak)


def solution(mesh):
    return jax.shard_map(
        functools.partial(shards, mesh.shape["section"]),
        mesh=mesh,
        in_specs=(
            P("section", None, "tp"),
            P("section", "tp", None),
            P("tp", None),
            P(),
            P("section"),
            P(None, "tp"),
        ),
        out_specs=(P("section", "tp", None), P("section", None, "tp"), P("section")),
        check_vma=False,
    )
```

```python
import functools
import jax
import jax.numpy as jnp
from jax import lax
from jax.experimental import pallas as pl
from jax.experimental.pallas import tpu as pltpu
from jax.sharding import PartitionSpec as P

epsilon = 1e-05
ceiling = 448.0

TP = 32
CHIPS = 16
ROWS = 8
TOK = 128
D = 8192
HALF = 4096
TAIL = 128
f32 = jnp.float32
bf16 = jnp.bfloat16


def across(x, d):
    return lax.ppermute(x, "tp", [(i, i ^ (2 * d)) for i in range(TP)])


def other_core(x):
    return lax.ppermute(x, "tp", [(i, i ^ 1) for i in range(TP)])


def next_section(x, sections):
    pairs = []
    for s in range(sections):
        shift = 16 if s % 4 == 3 else 0
        for t in range(TP):
            pairs.append((s * TP + t, ((s + 1) % sections) * TP + (t ^ shift)))
    return lax.ppermute(x, ("section", "tp"), pairs)


def shuffle(z):
    row = lax.broadcasted_iota(jnp.int32, (TOK, TOK), 0)
    col = lax.broadcasted_iota(jnp.int32, (TOK, TOK), 1)
    return jnp.where((row ^ (z * ROWS)) == col, 1.0, 0.0).astype(bf16)


N_TILE = 2048


def out_proj_body(ids, heads, weight, resid, out, rows):
    z = ids[0]
    core = ids[1]

    @pl.when(pl.program_id(0) == 0)
    def _():
        rows[...] = jnp.dot(shuffle(z), heads[...], preferred_element_type=f32).astype(bf16)

    product = jnp.dot(rows[...], weight[...], preferred_element_type=f32)
    out[...] = product.astype(out.dtype)
    mine = resid[...].astype(f32)
    zero = jnp.zeros_like(mine)
    eight = jnp.where(core == 0, jnp.concatenate([mine, zero], 0), jnp.concatenate([zero, mine], 0))
    out[0:ROWS, :] = (product[0:ROWS, :] + eight).astype(out.dtype)


def out_proj(ids, which, heads, weight, resid, dtype):
    tiles = HALF // N_TILE
    return pl.pallas_call(
        out_proj_body,
        out_shape=jax.ShapeDtypeStruct((TOK, HALF), dtype),
        grid_spec=pltpu.PrefetchScalarGridSpec(
            num_scalar_prefetch=1,
            grid=(tiles,),
            in_specs=[
                pl.BlockSpec((TOK, 256), lambda i, ids: (0, 0)),
                pl.BlockSpec((256, N_TILE), lambda i, ids: (0, ids[which] * tiles + i)),
                pl.BlockSpec((4, N_TILE), lambda i, ids: (0, ids[which] * tiles + i)),
            ],
            out_specs=pl.BlockSpec((TOK, N_TILE), lambda i, ids: (0, i)),
            scratch_shapes=[pltpu.VMEM((TOK, 256), bf16)],
        ),
        name="out_proj",
    )(ids, heads, weight, resid)


def cast_body(ids, own, twin, gain, peak_in, payload, peaks):
    wide = own[...].astype(f32)
    wide_twin = twin[...].astype(f32)
    total = jnp.sum(wide * wide, axis=-1, keepdims=True) + jnp.sum(wide_twin * wide_twin, axis=-1, keepdims=True)
    normed = wide * lax.rsqrt(total / D + epsilon) * gain[...].astype(f32)
    unit = jnp.full((ROWS, TAIL), peak_in[0] / ceiling, f32).astype(bf16)
    payload[:, 0:HALF] = jnp.clip(normed / unit[:, 0:1].astype(f32), -ceiling, ceiling).astype(bf16)
    payload[:, HALF:] = unit
    peak = jnp.max(jnp.max(jnp.abs(normed), axis=1, keepdims=True), axis=0, keepdims=True)
    peak = jnp.broadcast_to(peak, (ROWS, TAIL))
    high = peak.astype(bf16)
    low = (peak - high.astype(f32)).astype(bf16)
    lane = lax.broadcasted_iota(jnp.int32, (ROWS, TAIL), 1)
    peaks[...] = jnp.where(lane == 0, high.astype(f32), low.astype(f32)).astype(bf16)


def cast(ids, own, twin, gain, prior_peak):
    return pl.pallas_call(
        cast_body,
        out_shape=(
            jax.ShapeDtypeStruct((ROWS, HALF + TAIL), bf16),
            jax.ShapeDtypeStruct((ROWS, TAIL), bf16),
        ),
        grid_spec=pltpu.PrefetchScalarGridSpec(
            num_scalar_prefetch=1,
            grid=(1,),
            in_specs=[
                pl.BlockSpec((ROWS, HALF), lambda i, ids: (0, 0)),
                pl.BlockSpec((ROWS, HALF), lambda i, ids: (0, 0)),
                pl.BlockSpec((1, HALF), lambda i, ids: (0, ids[1])),
                pl.BlockSpec(memory_space=pltpu.SMEM),
            ],
            out_specs=[
                pl.BlockSpec((ROWS, HALF + TAIL), lambda i, ids: (0, 0)),
                pl.BlockSpec((ROWS, TAIL), lambda i, ids: (0, 0)),
            ],
        ),
        name="cast",
    )(ids, own, twin, gain.reshape(1, D), prior_peak)


K_TILE = 2048


def first_half_body(ids, weight, a, out):
    part = lax.dot_general(weight[...], a[...], (((1,), (1,)), ((), ())), preferred_element_type=f32)

    @pl.when(pl.program_id(0) == 0)
    def _():
        out[...] = part

    @pl.when(pl.program_id(0) > 0)
    def _():
        out[...] += part


def first_half(ids, weight, a):
    steps = HALF // K_TILE
    n = weight.shape[0]
    return pl.pallas_call(
        first_half_body,
        out_shape=jax.ShapeDtypeStruct((n, TOK), f32),
        grid_spec=pltpu.PrefetchScalarGridSpec(
            num_scalar_prefetch=1,
            grid=(steps,),
            in_specs=[
                pl.BlockSpec((n, K_TILE), lambda i, ids: (0, ids[1] * steps + i)),
                pl.BlockSpec((TOK, K_TILE), lambda i, ids: (0, i)),
            ],
            out_specs=pl.BlockSpec((n, TOK), lambda i, ids: (0, 0)),
        ),
        name="first_half",
    )(ids, weight, a)


def both_parts(tail):
    wide = tail.astype(f32)
    return wide[:, 0:1] + wide[:, 1:2]


def second_half_body(ids, weight, a, start, unit, tail, tail_twin, out, peak, acc):
    i = pl.program_id(0)
    part = lax.dot_general(weight[...], a[...], (((1,), (1,)), ((), ())), preferred_element_type=f32)

    @pl.when(i == 0)
    def _():
        acc[...] = start[...] + part

    @pl.when(i > 0)
    def _():
        acc[...] += part

    @pl.when(i == pl.num_programs(0) - 1)
    def _():
        scaled = (acc[...] * unit[0:1, 0:1].astype(f32)).astype(bf16)
        out[...] = jnp.dot(scaled, shuffle(ids[3]), preferred_element_type=f32).astype(bf16)
        ends = jnp.maximum(both_parts(tail[...]), both_parts(tail_twin[...]))
        peak[0] = jnp.max(ends)


def second_half(ids, weight, a, start, unit, twin):
    steps = HALF // K_TILE
    n = weight.shape[0]
    return pl.pallas_call(
        second_half_body,
        out_shape=(jax.ShapeDtypeStruct((n, TOK), bf16), jax.ShapeDtypeStruct((1,), f32)),
        grid_spec=pltpu.PrefetchScalarGridSpec(
            num_scalar_prefetch=1,
            grid=(steps,),
            in_specs=[
                pl.BlockSpec((n, K_TILE), lambda i, ids: (0, ids[2] * steps + i)),
                pl.BlockSpec((TOK, K_TILE), lambda i, ids: (0, i)),
                pl.BlockSpec((n, TOK), lambda i, ids: (0, 0)),
                pl.BlockSpec((ROWS, TAIL), lambda i, ids: (0, HALF // TAIL)),
                pl.BlockSpec((TOK, TAIL), lambda i, ids: (0, HALF // TAIL)),
                pl.BlockSpec((TOK, TAIL), lambda i, ids: (0, HALF // TAIL)),
            ],
            out_specs=[
                pl.BlockSpec((n, TOK), lambda i, ids: (0, 0)),
                pl.BlockSpec(memory_space=pltpu.SMEM),
            ],
            scratch_shapes=[pltpu.VMEM((n, TOK), f32)],
        ),
        name="second_half",
    )(ids, weight, a, start, unit, twin, a)


def cat(*blocks):
    return jnp.concatenate(blocks, axis=0)


def split(x):
    return [x[k * ROWS : (k + 1) * ROWS] for k in range(x.shape[0] // ROWS)]


def reduce_rounds(kept, incoming):
    def send(d, *which):
        got = across(cat(*[p[o].astype(bf16) for o in which]), d)
        return [g.astype(f32) for g in split(got)]

    last = slice(15 * ROWS, 16 * ROWS)
    first_out = (kept[last] + incoming[last].astype(f32)).astype(bf16)
    first_out, kept, incoming = lax.optimization_barrier((first_out, kept, incoming))
    p = [k + i.astype(f32) for k, i in zip(split(kept), split(incoming))]
    a = across(first_out, 1).astype(f32)
    b13, b11, b7 = send(1, 13, 11, 7)
    p[14] = p[14] + a
    (b14,) = send(2, 14)
    c9, c5, c3 = send(1, 9, 5, 3)
    p[10] = p[10] + b11
    p[6] = p[6] + b7
    c10, c6 = send(2, 10, 6)
    p[12] = p[12] + b13 + b14
    (c12,) = send(4, 12)
    p[4] = p[4] + c5 + c6
    p[2] = p[2] + c3
    (d4,) = send(4, 4)
    (d2,) = send(2, 2)
    (d1,) = send(1, 1)
    p[8] = p[8] + c9 + c10 + c12
    (d8,) = send(8, 8)
    return p[0] + d1 + d2 + d4 + d8


def gather_rounds(own):
    b = {0: own}
    for d in (8, 4, 2, 1):
        b[d] = across(own, d)
    b[12] = across(b[8], 4)
    b[10], b[6] = split(across(cat(b[8], b[4]), 2))
    b[9], b[5], b[3] = split(across(cat(b[8], b[4], b[2]), 1))
    b[14] = across(b[12], 2)
    b[13], b[11], b[7] = split(across(cat(b[12], b[10], b[6]), 1))
    b[15] = across(b[14], 1)
    return cat(*[b[o] for o in range(CHIPS)])


def shards(sections, head_outputs, residual, out_weight, norm_gain, prior_peak, qkv_weight):
    heads = head_outputs[0]
    resid = residual[0]
    section = lax.axis_index("section")
    place = lax.axis_index("tp")
    z = place // 2
    core = place % 2
    label = z ^ jnp.where(section % 4 == 0, 8, 0)
    ids = jnp.stack([z, core, 1 - core, label]).astype(jnp.int32)

    outgoing = out_proj(ids, 2, heads, out_weight, resid, bf16)
    incoming = other_core(outgoing)
    kept = out_proj(ids, 1, heads, out_weight, resid, f32)
    own = lax.reduce_precision(reduce_rounds(kept, incoming), 8, 7).astype(bf16)
    twin = other_core(own)
    outbound, peaks = cast(ids, own, twin, norm_gain, prior_peak)
    arrived = next_section(outbound, sections)

    payload = jnp.concatenate([arrived[:, :HALF], peaks], axis=1)
    mine = gather_rounds(payload)
    theirs = other_core(mine)

    weight = qkv_weight.T
    started = first_half(ids, weight, mine)
    columns, group_peak = second_half(ids, weight, theirs, started, arrived, mine)
    projected = columns.T

    first_row = core == 0
    own_rows = jnp.where(first_row, own[0:4], own[4:8])
    twin_rows = jnp.where(first_row, twin[0:4], twin[4:8])
    stream = jnp.where(
        first_row,
        jnp.concatenate([own_rows, twin_rows], axis=1),
        jnp.concatenate([twin_rows, own_rows], axis=1),
    )
    return (stream[None], projected[None], group_peak)


def solution(mesh):
    return jax.shard_map(
        functools.partial(shards, mesh.shape["section"]),
        mesh=mesh,
        in_specs=(
            P("section", None, "tp"),
            P("section", "tp", None),
            P("tp", None),
            P(),
            P("section"),
            P(None, "tp"),
        ),
        out_specs=(P("section", "tp", None), P("section", None, "tp"), P("section")),
        check_vma=False,
    )
```

```python
import functools
import jax
import jax.numpy as jnp
from jax import lax
from jax.experimental import pallas as pl
from jax.experimental.pallas import tpu as pltpu
from jax.sharding import PartitionSpec as P

epsilon = 1e-05
ceiling = 448.0

TP = 32
CHIPS = 16
ROWS = 8
TOK = 128
D = 8192
HALF = 4096
TAIL = 128
f32 = jnp.float32
bf16 = jnp.bfloat16


def across(x, d):
    return lax.ppermute(x, "tp", [(i, i ^ (2 * d)) for i in range(TP)])


def other_core(x):
    return lax.ppermute(x, "tp", [(i, i ^ 1) for i in range(TP)])


def next_section(x, sections):
    pairs = []
    for s in range(sections):
        shift = 16 if s % 4 == 3 else 0
        for t in range(TP):
            pairs.append((s * TP + t, ((s + 1) % sections) * TP + (t ^ shift)))
    return lax.ppermute(x, ("section", "tp"), pairs)


def shuffle(z):
    row = lax.broadcasted_iota(jnp.int32, (TOK, TOK), 0)
    col = lax.broadcasted_iota(jnp.int32, (TOK, TOK), 1)
    return jnp.where((row ^ (z * ROWS)) == col, 1.0, 0.0).astype(bf16)


N_TILE = 2048


def out_proj_body(ids, heads, weight, resid, out, rows):
    z = ids[0]
    core = ids[1]

    @pl.when(pl.program_id(0) == 0)
    def _():
        rows[...] = jnp.dot(shuffle(z), heads[...], preferred_element_type=f32).astype(bf16)

    product = jnp.dot(rows[...], weight[...], preferred_element_type=f32)
    out[...] = product.astype(out.dtype)
    mine = resid[...].astype(f32)
    zero = jnp.zeros_like(mine)
    eight = jnp.where(core == 0, jnp.concatenate([mine, zero], 0), jnp.concatenate([zero, mine], 0))
    out[0:ROWS, :] = (product[0:ROWS, :] + eight).astype(out.dtype)


def out_proj(ids, which, heads, weight, resid, dtype):
    tiles = HALF // N_TILE
    return pl.pallas_call(
        out_proj_body,
        out_shape=jax.ShapeDtypeStruct((TOK, HALF), dtype),
        grid_spec=pltpu.PrefetchScalarGridSpec(
            num_scalar_prefetch=1,
            grid=(tiles,),
            in_specs=[
                pl.BlockSpec((TOK, 256), lambda i, ids: (0, 0)),
                pl.BlockSpec((256, N_TILE), lambda i, ids: (0, ids[which] * tiles + i)),
                pl.BlockSpec((4, N_TILE), lambda i, ids: (0, ids[which] * tiles + i)),
            ],
            out_specs=pl.BlockSpec((TOK, N_TILE), lambda i, ids: (0, i)),
            scratch_shapes=[pltpu.VMEM((TOK, 256), bf16)],
        ),
        compiler_params=pltpu.CompilerParams(vmem_limit_bytes=16 << 20),
        name="out_proj",
    )(ids, heads, weight, resid)


def cast_body(ids, own, twin, gain, peak_in, payload, peaks):
    wide = own[...].astype(f32)
    wide_twin = twin[...].astype(f32)
    total = jnp.sum(wide * wide, axis=-1, keepdims=True) + jnp.sum(wide_twin * wide_twin, axis=-1, keepdims=True)
    normed = wide * lax.rsqrt(total / D + epsilon) * gain[...].astype(f32)
    unit = jnp.full((ROWS, TAIL), peak_in[0] / ceiling, f32).astype(bf16)
    payload[:, 0:HALF] = jnp.clip(normed / unit[:, 0:1].astype(f32), -ceiling, ceiling).astype(bf16)
    payload[:, HALF:] = unit
    peak = jnp.max(jnp.max(jnp.abs(normed), axis=1, keepdims=True), axis=0, keepdims=True)
    peak = jnp.broadcast_to(peak, (ROWS, TAIL))
    high = peak.astype(bf16)
    low = (peak - high.astype(f32)).astype(bf16)
    lane = lax.broadcasted_iota(jnp.int32, (ROWS, TAIL), 1)
    peaks[...] = jnp.where(lane == 0, high.astype(f32), low.astype(f32)).astype(bf16)


def cast(ids, own, twin, gain, prior_peak):
    return pl.pallas_call(
        cast_body,
        out_shape=(
            jax.ShapeDtypeStruct((ROWS, HALF + TAIL), bf16),
            jax.ShapeDtypeStruct((ROWS, TAIL), bf16),
        ),
        grid_spec=pltpu.PrefetchScalarGridSpec(
            num_scalar_prefetch=1,
            grid=(1,),
            in_specs=[
                pl.BlockSpec(memory_space=pltpu.VMEM),
                pl.BlockSpec(memory_space=pltpu.VMEM),
                pl.BlockSpec((1, HALF), lambda i, ids: (0, ids[1])),
                pl.BlockSpec(memory_space=pltpu.SMEM),
            ],
            out_specs=[pl.BlockSpec(memory_space=pltpu.VMEM), pl.BlockSpec(memory_space=pltpu.VMEM)],
        ),
        compiler_params=pltpu.CompilerParams(vmem_limit_bytes=8 << 20),
        name="cast",
    )(ids, own, twin, gain.reshape(1, D), prior_peak)


def on_chip(x):
    return pltpu.with_memory_space_constraint(x, pltpu.VMEM)


def prefetch_body(source, target, sem):
    copy = pltpu.make_async_copy(source, target, sem)
    copy.start()
    copy.wait()


def prefetch(weight):
    return pl.pallas_call(
        prefetch_body,
        out_shape=jax.ShapeDtypeStruct(weight.shape, weight.dtype),
        in_specs=[pl.BlockSpec(memory_space=pltpu.HBM)],
        out_specs=pl.BlockSpec(memory_space=pltpu.VMEM),
        scratch_shapes=[pltpu.SemaphoreType.DMA],
        compiler_params=pltpu.CompilerParams(vmem_limit_bytes=8 << 20),
        name="prefetch",
    )(pltpu.with_memory_space_constraint(weight, pltpu.HBM))


K_TILE = 2048
NT_DIMS = (((1,), (1,)), ((), ()))


def half_product(weight, a, half):
    total = None
    for i in range(HALF // K_TILE):
        at = pl.multiple_of(half * HALF + i * K_TILE, K_TILE)
        tile = a[:, i * K_TILE : (i + 1) * K_TILE]
        part = lax.dot_general(weight[:, pl.ds(at, K_TILE)], tile, NT_DIMS, preferred_element_type=f32)
        total = part if total is None else total + part
    return total


def first_half_body(ids, weight, a, out):
    out[...] = half_product(weight, a, ids[1])


def first_half(ids, weight, a):
    return pl.pallas_call(
        first_half_body,
        out_shape=jax.ShapeDtypeStruct((weight.shape[0], TOK), f32),
        in_specs=[
            pl.BlockSpec(memory_space=pltpu.SMEM),
            pl.BlockSpec(memory_space=pltpu.VMEM),
            pl.BlockSpec(memory_space=pltpu.VMEM),
        ],
        out_specs=pl.BlockSpec(memory_space=pltpu.VMEM),
        compiler_params=pltpu.CompilerParams(vmem_limit_bytes=16 << 20),
        name="first_half",
    )(ids, on_chip(weight), a)


def both_parts(tail):
    wide = tail.astype(f32)
    return wide[:, 0:1] + wide[:, 1:2]


def second_half_body(ids, weight, a, start, arrived, twin, out, peak):
    total = start[...] + half_product(weight, a, ids[2])
    scaled = (total * arrived[0:1, HALF : HALF + 1].astype(f32)).astype(bf16)
    out[...] = jnp.dot(scaled, shuffle(ids[3]), preferred_element_type=f32).astype(bf16)
    peak[0] = jnp.max(jnp.maximum(both_parts(a[:, HALF:]), both_parts(twin[:, HALF:])))


def second_half(ids, weight, a, start, arrived, twin):
    return pl.pallas_call(
        second_half_body,
        out_shape=(jax.ShapeDtypeStruct((weight.shape[0], TOK), bf16), jax.ShapeDtypeStruct((1,), f32)),
        in_specs=[pl.BlockSpec(memory_space=pltpu.SMEM)] + [pl.BlockSpec(memory_space=pltpu.VMEM)] * 5,
        out_specs=[
            pl.BlockSpec(memory_space=pltpu.VMEM),
            pl.BlockSpec(memory_space=pltpu.SMEM),
        ],
        compiler_params=pltpu.CompilerParams(vmem_limit_bytes=16 << 20),
        name="second_half",
    )(ids, on_chip(weight), a, start, arrived, twin)


def cat(*blocks):
    return jnp.concatenate(blocks, axis=0)


def split(x):
    return [x[k * ROWS : (k + 1) * ROWS] for k in range(x.shape[0] // ROWS)]


def apart(first, *rest):
    return lax.optimization_barrier((first, *rest))


def packed(*blocks):
    return cat(*[b.astype(bf16) for b in blocks])


def unpacked(x):
    return [g.astype(f32) for g in split(x)]


def reduce_rounds(kept, incoming):
    def block(o):
        rows = slice(o * ROWS, (o + 1) * ROWS)
        return kept[rows] + incoming[rows].astype(f32)

    out15, kept, incoming = apart(block(15).astype(bf16), kept, incoming)
    a15 = across(out15, 1)
    out13, kept, incoming = apart(packed(block(13), block(11), block(7)), kept, incoming)
    a13 = across(out13, 1)
    out9, kept, incoming = apart(packed(block(9), block(5), block(3)), kept, incoming)
    a9 = across(out9, 1)
    out14, kept, incoming = apart(packed(block(14) + a15.astype(f32)), kept, incoming)
    a14 = across(out14, 2)
    b13, b11, b7 = unpacked(a13)
    out12, b11, b7, kept, incoming = apart(packed(block(12) + b13 + a14.astype(f32)), b11, b7, kept, incoming)
    a12 = across(out12, 4)
    out10, kept, incoming = apart(packed(block(10) + b11, block(6) + b7), kept, incoming)
    a10 = across(out10, 2)
    c9, c5, c3 = unpacked(a9)
    out2, out1, c9, c5, kept, incoming = apart(
        packed(block(2) + c3), packed(block(1)), c9, c5, kept, incoming
    )
    a2 = across(out2, 2)
    a1 = across(out1, 1)
    c10, c6 = unpacked(a10)
    out8, c5, c6, kept, incoming = apart(packed(block(8) + c9 + c10 + a12.astype(f32)), c5, c6, kept, incoming)
    a8 = across(out8, 8)
    a4 = across(packed(block(4) + c5 + c6), 4)
    return block(0) + a1.astype(f32) + a2.astype(f32) + a4.astype(f32) + a8.astype(f32)


def gather_rounds(own):
    b = {0: own}
    for d in (8, 4, 2, 1):
        b[d] = across(own, d)
    b[12] = across(b[8], 4)
    two = cat(b[8], b[4])
    b[10], b[6] = split(across(two, 2))
    b[9], b[5], b[3] = split(across(cat(b[8], b[4], b[2]), 1))
    b[14] = across(b[12], 2)
    b[13], b[11], b[7] = split(across(cat(b[12], b[10], b[6]), 1))
    b[15] = across(b[14], 1)
    return cat(*[b[o] for o in range(CHIPS)])


def shards(sections, head_outputs, residual, out_weight, norm_gain, prior_peak, qkv_weight):
    heads = head_outputs[0]
    resid = residual[0]
    section = lax.axis_index("section")
    place = lax.axis_index("tp")
    z = place // 2
    core = place % 2
    label = z ^ jnp.where(section % 4 == 0, 8, 0)
    ids = jnp.stack([z, core, 1 - core, label]).astype(jnp.int32)

    weight = prefetch(qkv_weight.T)
    heads, resid, out_weight = [pltpu.with_memory_space_constraint(v, pltpu.HBM) for v in (heads, resid, out_weight)]
    outgoing = out_proj(ids, 2, heads, out_weight, resid, bf16)
    incoming = other_core(outgoing)
    kept = out_proj(ids, 1, heads, out_weight, resid, f32)
    own = lax.reduce_precision(reduce_rounds(kept, incoming), 8, 7).astype(bf16)
    twin = other_core(own)
    outbound, peaks = cast(ids, own, twin, norm_gain, prior_peak)
    arrived = next_section(outbound, sections)

    payload = jnp.concatenate([arrived[:, :HALF], peaks], axis=1)
    mine = gather_rounds(payload)
    theirs = other_core(mine)

    started = first_half(ids, weight, mine)
    columns, group_peak = second_half(ids, weight, theirs, started, arrived, mine)
    projected = columns.T

    first_row = core == 0
    own_rows = jnp.where(first_row, own[0:4], own[4:8])
    twin_rows = jnp.where(first_row, twin[0:4], twin[4:8])
    stream = jnp.where(
        first_row,
        jnp.concatenate([own_rows, twin_rows], axis=1),
        jnp.concatenate([twin_rows, own_rows], axis=1),
    )
    return (stream[None], projected[None], group_peak)


def solution(mesh):
    return jax.shard_map(
        functools.partial(shards, mesh.shape["section"]),
        mesh=mesh,
        in_specs=(
            P("section", None, "tp"),
            P("section", "tp", None),
            P("tp", None),
            P(),
            P("section"),
            P(None, "tp"),
        ),
        out_specs=(P("section", "tp", None), P("section", None, "tp"), P("section")),
        check_vma=False,
    )
```

```python
import functools
import jax
import jax.numpy as jnp
from jax import lax
from jax.experimental import pallas as pl
from jax.experimental.pallas import tpu as pltpu
from jax.sharding import PartitionSpec as P

epsilon = 1e-05
ceiling = 448.0

TP = 32
CHIPS = 16
ROWS = 8
TOK = 128
D = 8192
HALF = 4096
TAIL = 128
f32 = jnp.float32
bf16 = jnp.bfloat16


def across(x, d):
    return lax.ppermute(x, "tp", [(i, i ^ (2 * d)) for i in range(TP)])


def other_core(x):
    return lax.ppermute(x, "tp", [(i, i ^ 1) for i in range(TP)])


def next_section(x, sections):
    pairs = []
    for s in range(sections):
        shift = 16 if s % 4 == 3 else 0
        for t in range(TP):
            pairs.append((s * TP + t, ((s + 1) % sections) * TP + (t ^ shift)))
    return lax.ppermute(x, ("section", "tp"), pairs)


def shuffle(z):
    row = lax.broadcasted_iota(jnp.int32, (TOK, TOK), 0)
    col = lax.broadcasted_iota(jnp.int32, (TOK, TOK), 1)
    return jnp.where((row ^ (z * ROWS)) == col, 1.0, 0.0).astype(bf16)


N_TILE = 2048


def out_proj_body(ids, heads, weight, resid, out, rows):
    z = ids[0]
    core = ids[1]

    @pl.when(pl.program_id(0) == 0)
    def _():
        rows[...] = jnp.dot(shuffle(z), heads[...], preferred_element_type=f32).astype(bf16)

    product = jnp.dot(rows[...], weight[...], preferred_element_type=f32)
    out[...] = product.astype(out.dtype)
    mine = resid[...].astype(f32)
    zero = jnp.zeros_like(mine)
    eight = jnp.where(core == 0, jnp.concatenate([mine, zero], 0), jnp.concatenate([zero, mine], 0))
    out[0:ROWS, :] = (product[0:ROWS, :] + eight).astype(out.dtype)


def out_proj(ids, which, heads, weight, resid, dtype):
    tiles = HALF // N_TILE
    return pl.pallas_call(
        out_proj_body,
        out_shape=jax.ShapeDtypeStruct((TOK, HALF), dtype),
        grid_spec=pltpu.PrefetchScalarGridSpec(
            num_scalar_prefetch=1,
            grid=(tiles,),
            in_specs=[
                pl.BlockSpec((TOK, 256), lambda i, ids: (0, 0)),
                pl.BlockSpec((256, N_TILE), lambda i, ids: (0, ids[which] * tiles + i)),
                pl.BlockSpec((4, N_TILE), lambda i, ids: (0, ids[which] * tiles + i)),
            ],
            out_specs=pl.BlockSpec((TOK, N_TILE), lambda i, ids: (0, i)),
            scratch_shapes=[pltpu.VMEM((TOK, 256), bf16)],
        ),
        compiler_params=pltpu.CompilerParams(vmem_limit_bytes=16 << 20),
        name="out_proj",
    )(ids, heads, weight, resid)


def cast_body(ids, own, twin, gain, peak_in, payload, peaks):
    wide = own[...].astype(f32)
    wide_twin = twin[...].astype(f32)
    total = jnp.sum(wide * wide, axis=-1, keepdims=True) + jnp.sum(wide_twin * wide_twin, axis=-1, keepdims=True)
    normed = wide * lax.rsqrt(total / D + epsilon) * gain[...].astype(f32)
    unit = jnp.full((ROWS, TAIL), peak_in[0] / ceiling, f32).astype(bf16)
    payload[:, 0:HALF] = jnp.clip(normed / unit[:, 0:1].astype(f32), -ceiling, ceiling).astype(bf16)
    payload[:, HALF:] = unit
    peak = jnp.max(jnp.max(jnp.abs(normed), axis=1, keepdims=True), axis=0, keepdims=True)
    peak = jnp.broadcast_to(peak, (ROWS, TAIL))
    high = peak.astype(bf16)
    low = (peak - high.astype(f32)).astype(bf16)
    lane = lax.broadcasted_iota(jnp.int32, (ROWS, TAIL), 1)
    peaks[...] = jnp.where(lane == 0, high.astype(f32), low.astype(f32)).astype(bf16)


def cast(ids, own, twin, gain, prior_peak):
    return pl.pallas_call(
        cast_body,
        out_shape=(
            jax.ShapeDtypeStruct((ROWS, HALF + TAIL), bf16),
            jax.ShapeDtypeStruct((ROWS, TAIL), bf16),
        ),
        grid_spec=pltpu.PrefetchScalarGridSpec(
            num_scalar_prefetch=1,
            grid=(1,),
            in_specs=[
                pl.BlockSpec(memory_space=pltpu.VMEM),
                pl.BlockSpec(memory_space=pltpu.VMEM),
                pl.BlockSpec((1, HALF), lambda i, ids: (0, ids[1])),
                pl.BlockSpec(memory_space=pltpu.SMEM),
            ],
            out_specs=[pl.BlockSpec(memory_space=pltpu.VMEM), pl.BlockSpec(memory_space=pltpu.VMEM)],
        ),
        compiler_params=pltpu.CompilerParams(vmem_limit_bytes=8 << 20),
        name="cast",
    )(ids, own, twin, gain.reshape(1, D), prior_peak)


def on_chip(x):
    return pltpu.with_memory_space_constraint(x, pltpu.VMEM)


def prefetch_body(source, target, sem):
    copy = pltpu.make_async_copy(source, target, sem)
    copy.start()
    copy.wait()


def prefetch(weight):
    return pl.pallas_call(
        prefetch_body,
        out_shape=jax.ShapeDtypeStruct(weight.shape, weight.dtype),
        in_specs=[pl.BlockSpec(memory_space=pltpu.HBM)],
        out_specs=pl.BlockSpec(memory_space=pltpu.VMEM),
        scratch_shapes=[pltpu.SemaphoreType.DMA],
        compiler_params=pltpu.CompilerParams(vmem_limit_bytes=8 << 20),
        name="prefetch",
    )(pltpu.with_memory_space_constraint(weight, pltpu.HBM))


K_TILE = 2048
NT_DIMS = (((1,), (1,)), ((), ()))


def half_product(weight, a, half):
    total = None
    for i in range(HALF // K_TILE):
        at = pl.multiple_of(half * HALF + i * K_TILE, K_TILE)
        tile = a[:, i * K_TILE : (i + 1) * K_TILE]
        part = lax.dot_general(weight[:, pl.ds(at, K_TILE)], tile, NT_DIMS, preferred_element_type=f32)
        total = part if total is None else total + part
    return total


def first_half_body(ids, weight, a, out):
    out[...] = half_product(weight, a, ids[1])


def first_half(ids, weight, a):
    return pl.pallas_call(
        first_half_body,
        out_shape=jax.ShapeDtypeStruct((weight.shape[0], TOK), f32),
        in_specs=[
            pl.BlockSpec(memory_space=pltpu.SMEM),
            pl.BlockSpec(memory_space=pltpu.VMEM),
            pl.BlockSpec(memory_space=pltpu.VMEM),
        ],
        out_specs=pl.BlockSpec(memory_space=pltpu.VMEM),
        compiler_params=pltpu.CompilerParams(vmem_limit_bytes=16 << 20),
        name="first_half",
    )(ids, on_chip(weight), a)


def both_parts(tail):
    wide = tail.astype(f32)
    return wide[:, 0:1] + wide[:, 1:2]


def second_half_body(ids, weight, a, start, arrived, twin, out, peak):
    total = start[...] + half_product(weight, a, ids[2])
    scaled = (total * arrived[0:1, HALF : HALF + 1].astype(f32)).astype(bf16)
    out[...] = jnp.dot(scaled, shuffle(ids[3]), preferred_element_type=f32).astype(bf16)
    peak[0] = jnp.max(jnp.maximum(both_parts(a[:, HALF:]), both_parts(twin[:, HALF:])))


def second_half(ids, weight, a, start, arrived, twin):
    return pl.pallas_call(
        second_half_body,
        out_shape=(jax.ShapeDtypeStruct((weight.shape[0], TOK), bf16), jax.ShapeDtypeStruct((1,), f32)),
        in_specs=[pl.BlockSpec(memory_space=pltpu.SMEM)] + [pl.BlockSpec(memory_space=pltpu.VMEM)] * 5,
        out_specs=[
            pl.BlockSpec(memory_space=pltpu.VMEM),
            pl.BlockSpec(memory_space=pltpu.SMEM),
        ],
        compiler_params=pltpu.CompilerParams(vmem_limit_bytes=16 << 20),
        name="second_half",
    )(ids, on_chip(weight), a, start, arrived, twin)


def cat(*blocks):
    return jnp.concatenate(blocks, axis=0)


def split(x):
    return [x[k * ROWS : (k + 1) * ROWS] for k in range(x.shape[0] // ROWS)]


def apart(first, *rest):
    return lax.optimization_barrier((first, *rest))


def packed(*blocks):
    return cat(*[b.astype(bf16) for b in blocks])


def reduce_rounds(kept, incoming):
    def block(o):
        rows = slice(o * ROWS, (o + 1) * ROWS)
        return kept[rows] + incoming[rows].astype(f32)

    out15, kept, incoming = apart(block(15).astype(bf16), kept, incoming)
    a15 = across(out15, 1)
    out13, kept, incoming = apart(packed(block(13), block(11), block(7)), kept, incoming)
    a13 = across(out13, 1)
    out14, kept, incoming = apart(packed(block(14) + a15.astype(f32)), kept, incoming)
    a14 = across(out14, 2)
    b13, b11, b7 = split(a13)
    out12, b11, b7, kept, incoming = apart(
        packed(block(12) + b13.astype(f32) + a14.astype(f32)), b11, b7, kept, incoming
    )
    a12 = across(out12, 4)
    out10, kept, incoming = apart(packed(block(10) + b11.astype(f32), block(6) + b7.astype(f32)), kept, incoming)
    a10 = across(out10, 2)
    out9, kept, incoming = apart(packed(block(9), block(5), block(3)), kept, incoming)
    a9 = across(out9, 1)
    c9, c5, c3 = split(a9)
    c10, c6 = split(a10)
    out8, c5, c3, c6, kept, incoming = apart(
        packed(block(8) + c9.astype(f32) + c10.astype(f32) + a12.astype(f32)), c5, c3, c6, kept, incoming
    )
    a8 = across(out8, 8)
    a4 = across(packed(block(4) + c5.astype(f32) + c6.astype(f32)), 4)
    a2 = across(packed(block(2) + c3.astype(f32)), 2)
    a1 = across(packed(block(1)), 1)
    return block(0) + a1.astype(f32) + a2.astype(f32) + a4.astype(f32) + a8.astype(f32)


def gather_rounds(own):
    b = {0: own}
    for d in (8, 4, 2, 1):
        b[d] = across(own, d)
    b[12] = across(b[8], 4)
    two = cat(b[8], b[4])
    b[10], b[6] = split(across(two, 2))
    b[9], b[5], b[3] = split(across(cat(b[8], b[4], b[2]), 1))
    b[14] = across(b[12], 2)
    b[13], b[11], b[7] = split(across(cat(b[12], b[10], b[6]), 1))
    b[15] = across(b[14], 1)
    return cat(*[b[o] for o in range(CHIPS)])


def shards(sections, head_outputs, residual, out_weight, norm_gain, prior_peak, qkv_weight):
    heads = head_outputs[0]
    resid = residual[0]
    section = lax.axis_index("section")
    place = lax.axis_index("tp")
    z = place // 2
    core = place % 2
    label = z ^ jnp.where(section % 4 == 0, 8, 0)
    ids = jnp.stack([z, core, 1 - core, label]).astype(jnp.int32)

    weight = prefetch(qkv_weight.T)
    heads, resid, out_weight = [pltpu.with_memory_space_constraint(v, pltpu.HBM) for v in (heads, resid, out_weight)]
    outgoing = out_proj(ids, 2, heads, out_weight, resid, bf16)
    incoming = other_core(outgoing)
    kept = out_proj(ids, 1, heads, out_weight, resid, f32)
    own = lax.reduce_precision(reduce_rounds(kept, incoming), 8, 7).astype(bf16)
    twin = other_core(own)
    outbound, peaks = cast(ids, own, twin, norm_gain, prior_peak)
    arrived = next_section(outbound, sections)

    payload = jnp.concatenate([arrived[:, :HALF], peaks], axis=1)
    mine = gather_rounds(payload)
    theirs = other_core(mine)

    started = first_half(ids, weight, mine)
    columns, group_peak = second_half(ids, weight, theirs, started, arrived, mine)
    projected = columns.T

    first_row = core == 0
    own_rows = jnp.where(first_row, own[0:4], own[4:8])
    twin_rows = jnp.where(first_row, twin[0:4], twin[4:8])
    stream = jnp.where(
        first_row,
        jnp.concatenate([own_rows, twin_rows], axis=1),
        jnp.concatenate([twin_rows, own_rows], axis=1),
    )
    return (stream[None], projected[None], group_peak)


def solution(mesh):
    return jax.shard_map(
        functools.partial(shards, mesh.shape["section"]),
        mesh=mesh,
        in_specs=(
            P("section", None, "tp"),
            P("section", "tp", None),
            P("tp", None),
            P(),
            P("section"),
            P(None, "tp"),
        ),
        out_specs=(P("section", "tp", None), P("section", None, "tp"), P("section")),
        check_vma=False,
    )
```

```python
import functools
import jax
import jax.numpy as jnp
from jax import lax
from jax.experimental import pallas as pl
from jax.experimental.pallas import tpu as pltpu
from jax.sharding import PartitionSpec as P

epsilon = 1e-05
ceiling = 448.0

TP = 32
CHIPS = 16
ROWS = 8
TOK = 128
D = 8192
HALF = 4096
TAIL = 128
f32 = jnp.float32
bf16 = jnp.bfloat16


def across(x, d):
    return lax.ppermute(x, "tp", [(i, i ^ (2 * d)) for i in range(TP)])


def other_core(x):
    return lax.ppermute(x, "tp", [(i, i ^ 1) for i in range(TP)])


def next_section(x, sections):
    pairs = []
    for s in range(sections):
        shift = 16 if s % 4 == 3 else 0
        for t in range(TP):
            pairs.append((s * TP + t, ((s + 1) % sections) * TP + (t ^ shift)))
    return lax.ppermute(x, ("section", "tp"), pairs)


def shuffle(z):
    row = lax.broadcasted_iota(jnp.int32, (TOK, TOK), 0)
    col = lax.broadcasted_iota(jnp.int32, (TOK, TOK), 1)
    return jnp.where((row ^ (z * ROWS)) == col, 1.0, 0.0).astype(bf16)


N_TILE = 2048


def out_proj_body(ids, heads, weight, resid, out, rows):
    z = ids[0]
    core = ids[1]

    @pl.when(pl.program_id(0) == 0)
    def _():
        rows[...] = jnp.dot(shuffle(z), heads[...], preferred_element_type=f32).astype(bf16)

    product = jnp.dot(rows[...], weight[...], preferred_element_type=f32)
    out[...] = product.astype(out.dtype)
    mine = resid[...].astype(f32)
    zero = jnp.zeros_like(mine)
    eight = jnp.where(core == 0, jnp.concatenate([mine, zero], 0), jnp.concatenate([zero, mine], 0))
    out[0:ROWS, :] = (product[0:ROWS, :] + eight).astype(out.dtype)


def out_proj(ids, which, heads, weight, resid, dtype):
    tiles = HALF // N_TILE
    return pl.pallas_call(
        out_proj_body,
        out_shape=jax.ShapeDtypeStruct((TOK, HALF), dtype),
        grid_spec=pltpu.PrefetchScalarGridSpec(
            num_scalar_prefetch=1,
            grid=(tiles,),
            in_specs=[
                pl.BlockSpec((TOK, 256), lambda i, ids: (0, 0)),
                pl.BlockSpec((256, N_TILE), lambda i, ids: (0, ids[which] * tiles + i)),
                pl.BlockSpec((4, N_TILE), lambda i, ids: (0, ids[which] * tiles + i)),
            ],
            out_specs=pl.BlockSpec((TOK, N_TILE), lambda i, ids: (0, i)),
            scratch_shapes=[pltpu.VMEM((TOK, 256), bf16)],
        ),
        compiler_params=pltpu.CompilerParams(vmem_limit_bytes=16 << 20),
        name="out_proj",
    )(ids, heads, weight, resid)


def cast_body(ids, own, twin, gain, peak_in, payload, peaks):
    wide = own[...].astype(f32)
    wide_twin = twin[...].astype(f32)
    total = jnp.sum(wide * wide, axis=-1, keepdims=True) + jnp.sum(wide_twin * wide_twin, axis=-1, keepdims=True)
    normed = wide * lax.rsqrt(total / D + epsilon) * gain[...].astype(f32)
    unit = jnp.full((ROWS, TAIL), peak_in[0] / ceiling, f32).astype(bf16)
    payload[:, 0:HALF] = jnp.clip(normed / unit[:, 0:1].astype(f32), -ceiling, ceiling).astype(bf16)
    payload[:, HALF:] = unit
    peak = jnp.max(jnp.max(jnp.abs(normed), axis=1, keepdims=True), axis=0, keepdims=True)
    peak = jnp.broadcast_to(peak, (ROWS, TAIL))
    high = peak.astype(bf16)
    low = (peak - high.astype(f32)).astype(bf16)
    lane = lax.broadcasted_iota(jnp.int32, (ROWS, TAIL), 1)
    peaks[...] = jnp.where(lane == 0, high.astype(f32), low.astype(f32)).astype(bf16)


def cast(ids, own, twin, gain, prior_peak):
    return pl.pallas_call(
        cast_body,
        out_shape=(
            jax.ShapeDtypeStruct((ROWS, HALF + TAIL), bf16),
            jax.ShapeDtypeStruct((ROWS, TAIL), bf16),
        ),
        grid_spec=pltpu.PrefetchScalarGridSpec(
            num_scalar_prefetch=1,
            grid=(1,),
            in_specs=[
                pl.BlockSpec(memory_space=pltpu.VMEM),
                pl.BlockSpec(memory_space=pltpu.VMEM),
                pl.BlockSpec((1, HALF), lambda i, ids: (0, ids[1])),
                pl.BlockSpec(memory_space=pltpu.SMEM),
            ],
            out_specs=[pl.BlockSpec(memory_space=pltpu.VMEM), pl.BlockSpec(memory_space=pltpu.VMEM)],
        ),
        compiler_params=pltpu.CompilerParams(vmem_limit_bytes=8 << 20),
        name="cast",
    )(ids, own, twin, gain.reshape(1, D), prior_peak)


def on_chip(x):
    return pltpu.with_memory_space_constraint(x, pltpu.VMEM)


def prefetch_body(source, target, sem):
    copy = pltpu.make_async_copy(source, target, sem)
    copy.start()
    copy.wait()


def prefetch(weight):
    return pl.pallas_call(
        prefetch_body,
        out_shape=jax.ShapeDtypeStruct(weight.shape, weight.dtype),
        in_specs=[pl.BlockSpec(memory_space=pltpu.HBM)],
        out_specs=pl.BlockSpec(memory_space=pltpu.VMEM),
        scratch_shapes=[pltpu.SemaphoreType.DMA],
        compiler_params=pltpu.CompilerParams(vmem_limit_bytes=8 << 20),
        name="prefetch",
    )(pltpu.with_memory_space_constraint(weight, pltpu.HBM))


K_TILE = 2048
NT_DIMS = (((1,), (1,)), ((), ()))


def half_product(weight, a, half):
    total = None
    for i in range(HALF // K_TILE):
        at = pl.multiple_of(half * HALF + i * K_TILE, K_TILE)
        tile = a[:, i * K_TILE : (i + 1) * K_TILE]
        part = lax.dot_general(weight[:, pl.ds(at, K_TILE)], tile, NT_DIMS, preferred_element_type=f32)
        total = part if total is None else total + part
    return total


def first_half_body(ids, weight, a, out):
    out[...] = half_product(weight, a, ids[1])


def first_half(ids, weight, a):
    return pl.pallas_call(
        first_half_body,
        out_shape=jax.ShapeDtypeStruct((weight.shape[0], TOK), f32),
        in_specs=[
            pl.BlockSpec(memory_space=pltpu.SMEM),
            pl.BlockSpec(memory_space=pltpu.VMEM),
            pl.BlockSpec(memory_space=pltpu.VMEM),
        ],
        out_specs=pl.BlockSpec(memory_space=pltpu.VMEM),
        compiler_params=pltpu.CompilerParams(vmem_limit_bytes=16 << 20),
        name="first_half",
    )(ids, on_chip(weight), a)


def both_parts(tail):
    wide = tail.astype(f32)
    return wide[:, 0:1] + wide[:, 1:2]


def second_half_body(ids, weight, a, start, arrived, twin, out, peak):
    total = start[...] + half_product(weight, a, ids[2])
    scaled = (total * arrived[0:1, HALF : HALF + 1].astype(f32)).astype(bf16)
    out[...] = jnp.dot(scaled, shuffle(ids[3]), preferred_element_type=f32).astype(bf16)
    peak[0] = jnp.max(jnp.maximum(both_parts(a[:, HALF:]), both_parts(twin[:, HALF:])))


def second_half(ids, weight, a, start, arrived, twin):
    return pl.pallas_call(
        second_half_body,
        out_shape=(jax.ShapeDtypeStruct((weight.shape[0], TOK), bf16), jax.ShapeDtypeStruct((1,), f32)),
        in_specs=[pl.BlockSpec(memory_space=pltpu.SMEM)] + [pl.BlockSpec(memory_space=pltpu.VMEM)] * 5,
        out_specs=[
            pl.BlockSpec(memory_space=pltpu.VMEM),
            pl.BlockSpec(memory_space=pltpu.SMEM),
        ],
        compiler_params=pltpu.CompilerParams(vmem_limit_bytes=16 << 20),
        name="second_half",
    )(ids, on_chip(weight), a, start, arrived, twin)


def cat(*blocks):
    return jnp.concatenate(blocks, axis=0)


def split(x):
    return [x[k * ROWS : (k + 1) * ROWS] for k in range(x.shape[0] // ROWS)]


def apart(first, *rest):
    return lax.optimization_barrier((first, *rest))


def packed(*blocks):
    return cat(*[b.astype(bf16) for b in blocks])


def reduce_rounds(kept, incoming):
    def block(o):
        rows = slice(o * ROWS, (o + 1) * ROWS)
        return kept[rows] + incoming[rows].astype(f32)

    out15, kept, incoming = apart(block(15).astype(bf16), kept, incoming)
    a15 = across(out15, 1)
    out13, kept, incoming = apart(packed(block(13), block(11), block(7)), kept, incoming)
    a13 = across(out13, 1)
    out9, kept, incoming = apart(packed(block(9), block(5), block(3)), kept, incoming)
    a9 = across(out9, 1)
    out14, kept, incoming = apart(packed(block(14) + a15.astype(f32)), kept, incoming)
    a14 = across(out14, 2)
    b13, b11, b7 = split(a13)
    out10, b13, kept, incoming = apart(
        packed(block(10) + b11.astype(f32), block(6) + b7.astype(f32)), b13, kept, incoming
    )
    a10 = across(out10, 2)
    out12, kept, incoming = apart(packed(block(12) + b13.astype(f32) + a14.astype(f32)), kept, incoming)
    a12 = across(out12, 4)
    c9, c5, c3 = split(a9)
    out1, out2, c9, c5, kept, incoming = apart(
        packed(block(1)), packed(block(2) + c3.astype(f32)), c9, c5, kept, incoming
    )
    a1 = across(out1, 1)
    a2 = across(out2, 2)
    c10, c6 = split(a10)
    out4, c9, c10, kept, incoming = apart(
        packed(block(4) + c5.astype(f32) + c6.astype(f32)), c9, c10, kept, incoming
    )
    a4 = across(out4, 4)
    a8 = across(packed(block(8) + c9.astype(f32) + c10.astype(f32) + a12.astype(f32)), 8)
    return block(0) + a1.astype(f32) + a2.astype(f32) + a4.astype(f32) + a8.astype(f32)


def gather_rounds(own):
    b = {0: own}
    for d in (8, 4, 2, 1):
        b[d] = across(own, d)
    b[12] = across(b[8], 4)
    two = cat(b[8], b[4])
    b[10], b[6] = split(across(two, 2))
    b[9], b[5], b[3] = split(across(cat(b[8], b[4], b[2]), 1))
    b[14] = across(b[12], 2)
    b[13], b[11], b[7] = split(across(cat(b[12], b[10], b[6]), 1))
    b[15] = across(b[14], 1)
    return cat(*[b[o] for o in range(CHIPS)])


def shards(sections, head_outputs, residual, out_weight, norm_gain, prior_peak, qkv_weight):
    heads = head_outputs[0]
    resid = residual[0]
    section = lax.axis_index("section")
    place = lax.axis_index("tp")
    z = place // 2
    core = place % 2
    label = z ^ jnp.where(section % 4 == 0, 8, 0)
    ids = jnp.stack([z, core, 1 - core, label]).astype(jnp.int32)

    weight = prefetch(qkv_weight.T)
    heads, resid, out_weight = [pltpu.with_memory_space_constraint(v, pltpu.HBM) for v in (heads, resid, out_weight)]
    outgoing = out_proj(ids, 2, heads, out_weight, resid, bf16)
    incoming = other_core(outgoing)
    kept = out_proj(ids, 1, heads, out_weight, resid, f32)
    own = lax.reduce_precision(reduce_rounds(kept, incoming), 8, 7).astype(bf16)
    twin = other_core(own)
    outbound, peaks = cast(ids, own, twin, norm_gain, prior_peak)
    arrived = next_section(outbound, sections)

    payload = jnp.concatenate([arrived[:, :HALF], peaks], axis=1)
    mine = gather_rounds(payload)
    theirs = other_core(mine)

    started = first_half(ids, weight, mine)
    columns, group_peak = second_half(ids, weight, theirs, started, arrived, mine)
    projected = columns.T

    first_row = core == 0
    own_rows = jnp.where(first_row, own[0:4], own[4:8])
    twin_rows = jnp.where(first_row, twin[0:4], twin[4:8])
    stream = jnp.where(
        first_row,
        jnp.concatenate([own_rows, twin_rows], axis=1),
        jnp.concatenate([twin_rows, own_rows], axis=1),
    )
    return (stream[None], projected[None], group_peak)


def solution(mesh):
    return jax.shard_map(
        functools.partial(shards, mesh.shape["section"]),
        mesh=mesh,
        in_specs=(
            P("section", None, "tp"),
            P("section", "tp", None),
            P("tp", None),
            P(),
            P("section"),
            P(None, "tp"),
        ),
        out_specs=(P("section", "tp", None), P("section", None, "tp"), P("section")),
        check_vma=False,
    )
```

```python
import functools
import jax
import jax.numpy as jnp
from jax import lax
from jax.experimental import pallas as pl
from jax.experimental.pallas import tpu as pltpu
from jax.sharding import PartitionSpec as P

epsilon = 1e-05
ceiling = 448.0

TP = 32
CHIPS = 16
ROWS = 8
TOK = 128
D = 8192
HALF = 4096
TAIL = 128
f32 = jnp.float32
bf16 = jnp.bfloat16


def across(x, d):
    return lax.ppermute(x, "tp", [(i, i ^ (2 * d)) for i in range(TP)])


def other_core(x):
    return lax.ppermute(x, "tp", [(i, i ^ 1) for i in range(TP)])


def next_section(x, sections):
    pairs = []
    for s in range(sections):
        shift = 16 if s % 4 == 3 else 0
        for t in range(TP):
            pairs.append((s * TP + t, ((s + 1) % sections) * TP + (t ^ shift)))
    return lax.ppermute(x, ("section", "tp"), pairs)


def shuffle(z):
    row = lax.broadcasted_iota(jnp.int32, (TOK, TOK), 0)
    col = lax.broadcasted_iota(jnp.int32, (TOK, TOK), 1)
    return jnp.where((row ^ (z * ROWS)) == col, 1.0, 0.0).astype(bf16)


N_TILE = 2048


def out_proj_body(ids, heads, weight, resid, out, rows):
    z = ids[0]
    core = ids[1]

    @pl.when(pl.program_id(0) == 0)
    def _():
        rows[...] = jnp.dot(shuffle(z), heads[...], preferred_element_type=f32).astype(bf16)

    product = jnp.dot(rows[...], weight[...], preferred_element_type=f32)
    out[...] = product.astype(out.dtype)
    mine = resid[...].astype(f32)
    zero = jnp.zeros_like(mine)
    eight = jnp.where(core == 0, jnp.concatenate([mine, zero], 0), jnp.concatenate([zero, mine], 0))
    out[0:ROWS, :] = (product[0:ROWS, :] + eight).astype(out.dtype)


def out_proj(ids, which, heads, weight, resid, dtype):
    tiles = HALF // N_TILE
    return pl.pallas_call(
        out_proj_body,
        out_shape=jax.ShapeDtypeStruct((TOK, HALF), dtype),
        grid_spec=pltpu.PrefetchScalarGridSpec(
            num_scalar_prefetch=1,
            grid=(tiles,),
            in_specs=[
                pl.BlockSpec((TOK, 256), lambda i, ids: (0, 0)),
                pl.BlockSpec((256, N_TILE), lambda i, ids: (0, ids[which] * tiles + i)),
                pl.BlockSpec((4, N_TILE), lambda i, ids: (0, ids[which] * tiles + i)),
            ],
            out_specs=pl.BlockSpec((TOK, N_TILE), lambda i, ids: (0, i)),
            scratch_shapes=[pltpu.VMEM((TOK, 256), bf16)],
        ),
        compiler_params=pltpu.CompilerParams(vmem_limit_bytes=16 << 20),
        name="out_proj",
    )(ids, heads, weight, resid)


def cast_body(ids, own, twin, gain, peak_in, payload, peaks):
    wide = own[...].astype(f32)
    wide_twin = twin[...].astype(f32)
    total = jnp.sum(wide * wide, axis=-1, keepdims=True) + jnp.sum(wide_twin * wide_twin, axis=-1, keepdims=True)
    normed = wide * lax.rsqrt(total / D + epsilon) * gain[...].astype(f32)
    unit = jnp.full((ROWS, TAIL), peak_in[0] / ceiling, f32).astype(bf16)
    payload[:, 0:HALF] = jnp.clip(normed / unit[:, 0:1].astype(f32), -ceiling, ceiling).astype(bf16)
    payload[:, HALF:] = unit
    peak = jnp.max(jnp.max(jnp.abs(normed), axis=1, keepdims=True), axis=0, keepdims=True)
    peak = jnp.broadcast_to(peak, (ROWS, TAIL))
    high = peak.astype(bf16)
    low = (peak - high.astype(f32)).astype(bf16)
    lane = lax.broadcasted_iota(jnp.int32, (ROWS, TAIL), 1)
    peaks[...] = jnp.where(lane == 0, high.astype(f32), low.astype(f32)).astype(bf16)


def cast(ids, own, twin, gain, prior_peak):
    return pl.pallas_call(
        cast_body,
        out_shape=(
            jax.ShapeDtypeStruct((ROWS, HALF + TAIL), bf16),
            jax.ShapeDtypeStruct((ROWS, TAIL), bf16),
        ),
        grid_spec=pltpu.PrefetchScalarGridSpec(
            num_scalar_prefetch=1,
            grid=(1,),
            in_specs=[
                pl.BlockSpec(memory_space=pltpu.VMEM),
                pl.BlockSpec(memory_space=pltpu.VMEM),
                pl.BlockSpec((1, HALF), lambda i, ids: (0, ids[1])),
                pl.BlockSpec(memory_space=pltpu.SMEM),
            ],
            out_specs=[pl.BlockSpec(memory_space=pltpu.VMEM), pl.BlockSpec(memory_space=pltpu.VMEM)],
        ),
        compiler_params=pltpu.CompilerParams(vmem_limit_bytes=8 << 20),
        name="cast",
    )(ids, own, twin, gain.reshape(1, D), prior_peak)


def on_chip(x):
    return pltpu.with_memory_space_constraint(x, pltpu.VMEM)


def prefetch_body(source, target, sem):
    copy = pltpu.make_async_copy(source, target, sem)
    copy.start()
    copy.wait()


def prefetch(weight):
    return pl.pallas_call(
        prefetch_body,
        out_shape=jax.ShapeDtypeStruct(weight.shape, weight.dtype),
        in_specs=[pl.BlockSpec(memory_space=pltpu.HBM)],
        out_specs=pl.BlockSpec(memory_space=pltpu.VMEM),
        scratch_shapes=[pltpu.SemaphoreType.DMA],
        compiler_params=pltpu.CompilerParams(vmem_limit_bytes=8 << 20),
        name="prefetch",
    )(pltpu.with_memory_space_constraint(weight, pltpu.HBM))


K_TILE = 2048
NT_DIMS = (((1,), (1,)), ((), ()))


def half_product(weight, a, half):
    total = None
    for i in range(HALF // K_TILE):
        at = pl.multiple_of(half * HALF + i * K_TILE, K_TILE)
        tile = a[:, i * K_TILE : (i + 1) * K_TILE]
        part = lax.dot_general(weight[:, pl.ds(at, K_TILE)], tile, NT_DIMS, preferred_element_type=f32)
        total = part if total is None else total + part
    return total


def first_half_body(ids, weight, a, out):
    out[...] = half_product(weight, a, ids[1])


def first_half(ids, weight, a):
    return pl.pallas_call(
        first_half_body,
        out_shape=jax.ShapeDtypeStruct((weight.shape[0], TOK), f32),
        in_specs=[
            pl.BlockSpec(memory_space=pltpu.SMEM),
            pl.BlockSpec(memory_space=pltpu.VMEM),
            pl.BlockSpec(memory_space=pltpu.VMEM),
        ],
        out_specs=pl.BlockSpec(memory_space=pltpu.VMEM),
        compiler_params=pltpu.CompilerParams(vmem_limit_bytes=16 << 20),
        name="first_half",
    )(ids, on_chip(weight), a)


def both_parts(tail):
    wide = tail.astype(f32)
    return wide[:, 0:1] + wide[:, 1:2]


def second_half_body(ids, weight, a, start, arrived, twin, out, peak):
    total = start[...] + half_product(weight, a, ids[2])
    scaled = (total * arrived[0:1, HALF : HALF + 1].astype(f32)).astype(bf16)
    out[...] = jnp.dot(scaled, shuffle(ids[3]), preferred_element_type=f32).astype(bf16)
    peak[0] = jnp.max(jnp.maximum(both_parts(a[:, HALF:]), both_parts(twin[:, HALF:])))


def second_half(ids, weight, a, start, arrived, twin):
    return pl.pallas_call(
        second_half_body,
        out_shape=(jax.ShapeDtypeStruct((weight.shape[0], TOK), bf16), jax.ShapeDtypeStruct((1,), f32)),
        in_specs=[pl.BlockSpec(memory_space=pltpu.SMEM)] + [pl.BlockSpec(memory_space=pltpu.VMEM)] * 5,
        out_specs=[
            pl.BlockSpec(memory_space=pltpu.VMEM),
            pl.BlockSpec(memory_space=pltpu.SMEM),
        ],
        compiler_params=pltpu.CompilerParams(vmem_limit_bytes=16 << 20),
        name="second_half",
    )(ids, on_chip(weight), a, start, arrived, twin)


def cat(*blocks):
    return jnp.concatenate(blocks, axis=0)


def split(x):
    return [x[k * ROWS : (k + 1) * ROWS] for k in range(x.shape[0] // ROWS)]


def apart(first, *rest):
    return lax.optimization_barrier((first, *rest))


def packed(*blocks):
    return cat(*[b.astype(bf16) for b in blocks])


def reduce_rounds(kept, incoming):
    def block(o):
        rows = slice(o * ROWS, (o + 1) * ROWS)
        return kept[rows] + incoming[rows].astype(f32)

    out15, kept, incoming = apart(block(15).astype(bf16), kept, incoming)
    a15 = across(out15, 1)
    out13, kept, incoming = apart(packed(block(13), block(11), block(7)), kept, incoming)
    a13 = across(out13, 1)
    out9, kept, incoming = apart(packed(block(9), block(5), block(3), block(1)), kept, incoming)
    a9 = across(out9, 1)
    out14, kept, incoming = apart(packed(block(14) + a15.astype(f32)), kept, incoming)
    a14 = across(out14, 2)
    b13, b11, b7 = split(a13)
    out10, b13, kept, incoming = apart(
        packed(block(10) + b11.astype(f32), block(6) + b7.astype(f32)), b13, kept, incoming
    )
    a10 = across(out10, 2)
    out12, kept, incoming = apart(packed(block(12) + b13.astype(f32) + a14.astype(f32)), kept, incoming)
    a12 = across(out12, 4)
    c9, c5, c3, a1 = split(a9)
    c10, c6 = split(a10)
    out4, c9, c10, kept, incoming = apart(
        packed(block(4) + c5.astype(f32) + c6.astype(f32)), c9, c10, kept, incoming
    )
    a4 = across(out4, 4)
    out8, c3, kept, incoming = apart(
        packed(block(8) + c9.astype(f32) + c10.astype(f32) + a12.astype(f32)), c3, kept, incoming
    )
    a8 = across(out8, 8)
    a2 = across(packed(block(2) + c3.astype(f32)), 2)
    return block(0) + a1.astype(f32) + a2.astype(f32) + a4.astype(f32) + a8.astype(f32)


def gather_rounds(own):
    b = {0: own}
    for d in (8, 4, 2, 1):
        b[d] = across(own, d)
    b[12] = across(b[8], 4)
    two = cat(b[8], b[4])
    b[10], b[6] = split(across(two, 2))
    b[9], b[5], b[3] = split(across(cat(b[8], b[4], b[2]), 1))
    b[14] = across(b[12], 2)
    b[13], b[11], b[7] = split(across(cat(b[12], b[10], b[6]), 1))
    b[15] = across(b[14], 1)
    return cat(*[b[o] for o in range(CHIPS)])


def shards(sections, head_outputs, residual, out_weight, norm_gain, prior_peak, qkv_weight):
    heads = head_outputs[0]
    resid = residual[0]
    section = lax.axis_index("section")
    place = lax.axis_index("tp")
    z = place // 2
    core = place % 2
    label = z ^ jnp.where(section % 4 == 0, 8, 0)
    ids = jnp.stack([z, core, 1 - core, label]).astype(jnp.int32)

    weight = prefetch(qkv_weight.T)
    heads, resid, out_weight = [pltpu.with_memory_space_constraint(v, pltpu.HBM) for v in (heads, resid, out_weight)]
    outgoing = out_proj(ids, 2, heads, out_weight, resid, bf16)
    incoming = other_core(outgoing)
    kept = out_proj(ids, 1, heads, out_weight, resid, f32)
    own = lax.reduce_precision(reduce_rounds(kept, incoming), 8, 7).astype(bf16)
    twin = other_core(own)
    outbound, peaks = cast(ids, own, twin, norm_gain, prior_peak)
    arrived = next_section(outbound, sections)

    payload = jnp.concatenate([arrived[:, :HALF], peaks], axis=1)
    mine = gather_rounds(payload)
    theirs = other_core(mine)

    started = first_half(ids, weight, mine)
    columns, group_peak = second_half(ids, weight, theirs, started, arrived, mine)
    projected = columns.T

    first_row = core == 0
    own_rows = jnp.where(first_row, own[0:4], own[4:8])
    twin_rows = jnp.where(first_row, twin[0:4], twin[4:8])
    stream = jnp.where(
        first_row,
        jnp.concatenate([own_rows, twin_rows], axis=1),
        jnp.concatenate([twin_rows, own_rows], axis=1),
    )
    return (stream[None], projected[None], group_peak)


def solution(mesh):
    return jax.shard_map(
        functools.partial(shards, mesh.shape["section"]),
        mesh=mesh,
        in_specs=(
            P("section", None, "tp"),
            P("section", "tp", None),
            P("tp", None),
            P(),
            P("section"),
            P(None, "tp"),
        ),
        out_specs=(P("section", "tp", None), P("section", None, "tp"), P("section")),
        check_vma=False,
    )
```

```python
import functools
import jax
import jax.numpy as jnp
from jax import lax
from jax.experimental import pallas as pl
from jax.experimental.pallas import tpu as pltpu
from jax.sharding import PartitionSpec as P

epsilon = 1e-05
ceiling = 448.0

TP = 32
CHIPS = 16
ROWS = 8
TOK = 128
D = 8192
HALF = 4096
TAIL = 128
f32 = jnp.float32
bf16 = jnp.bfloat16


def across(x, d):
    return lax.ppermute(x, "tp", [(i, i ^ (2 * d)) for i in range(TP)])


def other_core(x):
    return lax.ppermute(x, "tp", [(i, i ^ 1) for i in range(TP)])


def next_section(x, sections):
    pairs = []
    for s in range(sections):
        shift = 16 if s % 4 == 3 else 0
        for t in range(TP):
            pairs.append((s * TP + t, ((s + 1) % sections) * TP + (t ^ shift)))
    return lax.ppermute(x, ("section", "tp"), pairs)


def shuffle(z):
    row = lax.broadcasted_iota(jnp.int32, (TOK, TOK), 0)
    col = lax.broadcasted_iota(jnp.int32, (TOK, TOK), 1)
    return jnp.where((row ^ (z * ROWS)) == col, 1.0, 0.0).astype(bf16)


N_TILE = 2048


def out_proj_body(ids, heads, weight, resid, out, rows):
    z = ids[0]
    core = ids[1]

    @pl.when(pl.program_id(0) == 0)
    def _():
        rows[...] = jnp.dot(shuffle(z), heads[...], preferred_element_type=f32).astype(bf16)

    product = jnp.dot(rows[...], weight[...], preferred_element_type=f32)
    out[...] = product.astype(out.dtype)
    mine = resid[...].astype(f32)
    zero = jnp.zeros_like(mine)
    eight = jnp.where(core == 0, jnp.concatenate([mine, zero], 0), jnp.concatenate([zero, mine], 0))
    out[0:ROWS, :] = (product[0:ROWS, :] + eight).astype(out.dtype)


def out_proj(ids, which, heads, weight, resid, dtype):
    tiles = HALF // N_TILE
    return pl.pallas_call(
        out_proj_body,
        out_shape=jax.ShapeDtypeStruct((TOK, HALF), dtype),
        grid_spec=pltpu.PrefetchScalarGridSpec(
            num_scalar_prefetch=1,
            grid=(tiles,),
            in_specs=[
                pl.BlockSpec((TOK, 256), lambda i, ids: (0, 0)),
                pl.BlockSpec((256, N_TILE), lambda i, ids: (0, ids[which] * tiles + i)),
                pl.BlockSpec((4, N_TILE), lambda i, ids: (0, ids[which] * tiles + i)),
            ],
            out_specs=pl.BlockSpec((TOK, N_TILE), lambda i, ids: (0, i)),
            scratch_shapes=[pltpu.VMEM((TOK, 256), bf16)],
        ),
        compiler_params=pltpu.CompilerParams(vmem_limit_bytes=16 << 20),
        name="out_proj",
    )(ids, heads, weight, resid)


def cast_body(ids, own, twin, gain, peak_in, payload, peaks):
    wide = own[...].astype(f32)
    wide_twin = twin[...].astype(f32)
    total = jnp.sum(wide * wide, axis=-1, keepdims=True) + jnp.sum(wide_twin * wide_twin, axis=-1, keepdims=True)
    normed = wide * lax.rsqrt(total / D + epsilon) * gain[...].astype(f32)
    unit = jnp.full((ROWS, TAIL), peak_in[0] / ceiling, f32).astype(bf16)
    payload[:, 0:HALF] = jnp.clip(normed / unit[:, 0:1].astype(f32), -ceiling, ceiling).astype(bf16)
    payload[:, HALF:] = unit
    peak = jnp.max(jnp.max(jnp.abs(normed), axis=1, keepdims=True), axis=0, keepdims=True)
    peak = jnp.broadcast_to(peak, (ROWS, TAIL))
    high = peak.astype(bf16)
    low = (peak - high.astype(f32)).astype(bf16)
    lane = lax.broadcasted_iota(jnp.int32, (ROWS, TAIL), 1)
    peaks[...] = jnp.where(lane == 0, high.astype(f32), low.astype(f32)).astype(bf16)


def cast(ids, own, twin, gain, prior_peak):
    return pl.pallas_call(
        cast_body,
        out_shape=(
            jax.ShapeDtypeStruct((ROWS, HALF + TAIL), bf16),
            jax.ShapeDtypeStruct((ROWS, TAIL), bf16),
        ),
        grid_spec=pltpu.PrefetchScalarGridSpec(
            num_scalar_prefetch=1,
            grid=(1,),
            in_specs=[
                pl.BlockSpec(memory_space=pltpu.VMEM),
                pl.BlockSpec(memory_space=pltpu.VMEM),
                pl.BlockSpec((1, HALF), lambda i, ids: (0, ids[1])),
                pl.BlockSpec(memory_space=pltpu.SMEM),
            ],
            out_specs=[pl.BlockSpec(memory_space=pltpu.VMEM), pl.BlockSpec(memory_space=pltpu.VMEM)],
        ),
        compiler_params=pltpu.CompilerParams(vmem_limit_bytes=8 << 20),
        name="cast",
    )(ids, own, twin, gain.reshape(1, D), prior_peak)


def on_chip(x):
    return pltpu.with_memory_space_constraint(x, pltpu.VMEM)


def prefetch_body(source, target, sem):
    copy = pltpu.make_async_copy(source, target, sem)
    copy.start()
    copy.wait()


def prefetch(weight):
    return pl.pallas_call(
        prefetch_body,
        out_shape=jax.ShapeDtypeStruct(weight.shape, weight.dtype),
        in_specs=[pl.BlockSpec(memory_space=pltpu.HBM)],
        out_specs=pl.BlockSpec(memory_space=pltpu.VMEM),
        scratch_shapes=[pltpu.SemaphoreType.DMA],
        compiler_params=pltpu.CompilerParams(vmem_limit_bytes=8 << 20),
        name="prefetch",
    )(pltpu.with_memory_space_constraint(weight, pltpu.HBM))


K_TILE = 2048
NT_DIMS = (((1,), (1,)), ((), ()))


def half_product(weight, a, half):
    total = None
    for i in range(HALF // K_TILE):
        at = pl.multiple_of(half * HALF + i * K_TILE, K_TILE)
        tile = a[:, i * K_TILE : (i + 1) * K_TILE]
        part = lax.dot_general(weight[:, pl.ds(at, K_TILE)], tile, NT_DIMS, preferred_element_type=f32)
        total = part if total is None else total + part
    return total


def first_half_body(ids, weight, a, out):
    out[...] = half_product(weight, a, ids[1])


def first_half(ids, weight, a):
    return pl.pallas_call(
        first_half_body,
        out_shape=jax.ShapeDtypeStruct((weight.shape[0], TOK), f32),
        in_specs=[
            pl.BlockSpec(memory_space=pltpu.SMEM),
            pl.BlockSpec(memory_space=pltpu.VMEM),
            pl.BlockSpec(memory_space=pltpu.VMEM),
        ],
        out_specs=pl.BlockSpec(memory_space=pltpu.VMEM),
        compiler_params=pltpu.CompilerParams(vmem_limit_bytes=16 << 20),
        name="first_half",
    )(ids, on_chip(weight), a)


def both_parts(tail):
    wide = tail.astype(f32)
    return wide[:, 0:1] + wide[:, 1:2]


def second_half_body(ids, weight, a, start, arrived, twin, out, peak):
    total = start[...] + half_product(weight, a, ids[2])
    scaled = (total * arrived[0:1, HALF : HALF + 1].astype(f32)).astype(bf16)
    out[...] = jnp.dot(scaled, shuffle(ids[3]), preferred_element_type=f32).astype(bf16)
    peak[0] = jnp.max(jnp.maximum(both_parts(a[:, HALF:]), both_parts(twin[:, HALF:])))


def second_half(ids, weight, a, start, arrived, twin):
    return pl.pallas_call(
        second_half_body,
        out_shape=(jax.ShapeDtypeStruct((weight.shape[0], TOK), bf16), jax.ShapeDtypeStruct((1,), f32)),
        in_specs=[pl.BlockSpec(memory_space=pltpu.SMEM)] + [pl.BlockSpec(memory_space=pltpu.VMEM)] * 5,
        out_specs=[
            pl.BlockSpec(memory_space=pltpu.VMEM),
            pl.BlockSpec(memory_space=pltpu.SMEM),
        ],
        compiler_params=pltpu.CompilerParams(vmem_limit_bytes=16 << 20),
        name="second_half",
    )(ids, on_chip(weight), a, start, arrived, twin)


def cat(*blocks):
    return jnp.concatenate(blocks, axis=0)


def split(x):
    return [x[k * ROWS : (k + 1) * ROWS] for k in range(x.shape[0] // ROWS)]


def apart(first, *rest):
    return lax.optimization_barrier((first, *rest))


def packed(*blocks):
    return cat(*[b.astype(bf16) for b in blocks])


def reduce_rounds(kept, incoming):
    def block(o):
        rows = slice(o * ROWS, (o + 1) * ROWS)
        return kept[rows] + incoming[rows].astype(f32)

    out15, kept, incoming = apart(block(15).astype(bf16), kept, incoming)
    a15 = across(out15, 1)
    out13, kept, incoming = apart(packed(block(13), block(11), block(7)), kept, incoming)
    a13 = across(out13, 1)
    out9, kept, incoming = apart(packed(block(9), block(5), block(3), block(1)), kept, incoming)
    a9 = across(out9, 1)
    out14, kept, incoming = apart(packed(block(14) + a15.astype(f32)), kept, incoming)
    a14 = across(out14, 2)
    b13, b11, b7 = split(a13)
    out10, b13, kept, incoming = apart(
        packed(block(10) + b11.astype(f32), block(6) + b7.astype(f32)), b13, kept, incoming
    )
    a10 = across(out10, 2)
    out12, kept, incoming = apart(packed(block(12) + b13.astype(f32) + a14.astype(f32)), kept, incoming)
    a12 = across(out12, 4)
    c9, c5, c3, a1 = split(a9)
    c10, c6 = split(a10)
    out4, c9, c10, kept, incoming = apart(
        packed(block(4) + c5.astype(f32) + c6.astype(f32)), c9, c10, kept, incoming
    )
    a4 = across(out4, 4)
    total8 = packed(block(8) + c9.astype(f32) + c10.astype(f32) + a12.astype(f32))
    out8, c3, kept, incoming = apart(total8, c3, kept, incoming)
    a8 = across(out8, 8)
    a2 = across(packed(block(2) + c3.astype(f32)), 2)
    return block(0) + a1.astype(f32) + a2.astype(f32) + a4.astype(f32) + a8.astype(f32)


def gather_rounds(own):
    b = {0: own}
    for d in (8, 4, 2):
        b[d] = across(own, d)
    b[12] = across(b[8], 4)
    two = cat(b[8], b[4])
    b[10], b[6] = split(across(two, 2))
    b[9], b[5], b[3], b[1] = split(across(cat(b[8], b[4], b[2], own), 1))
    b[14] = across(b[12], 2)
    b[13], b[11], b[7] = split(across(cat(b[12], b[10], b[6]), 1))
    b[15] = across(b[14], 1)
    return cat(*[b[o] for o in range(CHIPS)])


def shards(sections, head_outputs, residual, out_weight, norm_gain, prior_peak, qkv_weight):
    heads = head_outputs[0]
    resid = residual[0]
    section = lax.axis_index("section")
    place = lax.axis_index("tp")
    z = place // 2
    core = place % 2
    label = z ^ jnp.where(section % 4 == 0, 8, 0)
    ids = jnp.stack([z, core, 1 - core, label]).astype(jnp.int32)

    weight = prefetch(qkv_weight.T)
    heads, resid, out_weight = [pltpu.with_memory_space_constraint(v, pltpu.HBM) for v in (heads, resid, out_weight)]
    outgoing = out_proj(ids, 2, heads, out_weight, resid, bf16)
    incoming = other_core(outgoing)
    kept = out_proj(ids, 1, heads, out_weight, resid, f32)
    own = lax.reduce_precision(reduce_rounds(kept, incoming), 8, 7).astype(bf16)
    twin = other_core(own)
    outbound, peaks = cast(ids, own, twin, norm_gain, prior_peak)
    arrived = next_section(outbound, sections)

    payload = jnp.concatenate([arrived[:, :HALF], peaks], axis=1)
    mine = gather_rounds(payload)
    theirs = other_core(mine)

    started = first_half(ids, weight, mine)
    columns, group_peak = second_half(ids, weight, theirs, started, arrived, mine)
    projected = columns.T

    first_row = core == 0
    own_rows = jnp.where(first_row, own[0:4], own[4:8])
    twin_rows = jnp.where(first_row, twin[0:4], twin[4:8])
    stream = jnp.where(
        first_row,
        jnp.concatenate([own_rows, twin_rows], axis=1),
        jnp.concatenate([twin_rows, own_rows], axis=1),
    )
    return (stream[None], projected[None], group_peak)


def solution(mesh):
    return jax.shard_map(
        functools.partial(shards, mesh.shape["section"]),
        mesh=mesh,
        in_specs=(
            P("section", None, "tp"),
            P("section", "tp", None),
            P("tp", None),
            P(),
            P("section"),
            P(None, "tp"),
        ),
        out_specs=(P("section", "tp", None), P("section", None, "tp"), P("section")),
        check_vma=False,
    )
```

```python
import functools
import jax
import jax.numpy as jnp
from jax import lax
from jax.experimental import pallas as pl
from jax.experimental.pallas import tpu as pltpu
from jax.sharding import PartitionSpec as P

epsilon = 1e-05
ceiling = 448.0

TP = 32
CHIPS = 16
ROWS = 8
TOK = 128
D = 8192
HALF = 4096
TAIL = 128
f32 = jnp.float32
bf16 = jnp.bfloat16


def across(x, d):
    return lax.ppermute(x, "tp", [(i, i ^ (2 * d)) for i in range(TP)])


def other_core(x):
    return lax.ppermute(x, "tp", [(i, i ^ 1) for i in range(TP)])


def next_section(x, sections):
    pairs = []
    for s in range(sections):
        shift = 16 if s % 4 == 3 else 0
        for t in range(TP):
            pairs.append((s * TP + t, ((s + 1) % sections) * TP + (t ^ shift)))
    return lax.ppermute(x, ("section", "tp"), pairs)


def shuffle(z):
    row = lax.broadcasted_iota(jnp.int32, (TOK, TOK), 0)
    col = lax.broadcasted_iota(jnp.int32, (TOK, TOK), 1)
    return jnp.where((row ^ (z * ROWS)) == col, 1.0, 0.0).astype(bf16)


N_TILE = 2048


def out_proj_body(ids, heads, weight, resid, out, rows):
    z = ids[0]
    core = ids[1]

    @pl.when(pl.program_id(0) == 0)
    def _():
        rows[...] = jnp.dot(shuffle(z), heads[...], preferred_element_type=f32).astype(bf16)

    product = jnp.dot(rows[...], weight[...], preferred_element_type=f32)
    out[...] = product.astype(out.dtype)
    mine = resid[...].astype(f32)
    zero = jnp.zeros_like(mine)
    eight = jnp.where(core == 0, jnp.concatenate([mine, zero], 0), jnp.concatenate([zero, mine], 0))
    out[0:ROWS, :] = (product[0:ROWS, :] + eight).astype(out.dtype)


def out_proj(ids, which, heads, weight, resid, dtype):
    tiles = HALF // N_TILE
    return pl.pallas_call(
        out_proj_body,
        out_shape=jax.ShapeDtypeStruct((TOK, HALF), dtype),
        grid_spec=pltpu.PrefetchScalarGridSpec(
            num_scalar_prefetch=1,
            grid=(tiles,),
            in_specs=[
                pl.BlockSpec((TOK, 256), lambda i, ids: (0, 0)),
                pl.BlockSpec((256, N_TILE), lambda i, ids: (0, ids[which] * tiles + i)),
                pl.BlockSpec((4, N_TILE), lambda i, ids: (0, ids[which] * tiles + i)),
            ],
            out_specs=pl.BlockSpec((TOK, N_TILE), lambda i, ids: (0, i)),
            scratch_shapes=[pltpu.VMEM((TOK, 256), bf16)],
        ),
        compiler_params=pltpu.CompilerParams(vmem_limit_bytes=16 << 20),
        name="out_proj",
    )(ids, heads, weight, resid)


def cast_body(ids, own, twin, gain, peak_in, payload, peaks):
    wide = own[...].astype(f32)
    wide_twin = twin[...].astype(f32)
    total = jnp.sum(wide * wide, axis=-1, keepdims=True) + jnp.sum(wide_twin * wide_twin, axis=-1, keepdims=True)
    normed = wide * lax.rsqrt(total / D + epsilon) * gain[...].astype(f32)
    unit = jnp.full((ROWS, TAIL), peak_in[0] / ceiling, f32).astype(bf16)
    payload[:, 0:HALF] = jnp.clip(normed / unit[:, 0:1].astype(f32), -ceiling, ceiling).astype(bf16)
    payload[:, HALF:] = unit
    peak = jnp.max(jnp.max(jnp.abs(normed), axis=1, keepdims=True), axis=0, keepdims=True)
    peak = jnp.broadcast_to(peak, (ROWS, TAIL))
    high = peak.astype(bf16)
    low = (peak - high.astype(f32)).astype(bf16)
    lane = lax.broadcasted_iota(jnp.int32, (ROWS, TAIL), 1)
    peaks[...] = jnp.where(lane == 0, high.astype(f32), low.astype(f32)).astype(bf16)


def cast(ids, own, twin, gain, prior_peak):
    return pl.pallas_call(
        cast_body,
        out_shape=(
            jax.ShapeDtypeStruct((ROWS, HALF + TAIL), bf16),
            jax.ShapeDtypeStruct((ROWS, TAIL), bf16),
        ),
        grid_spec=pltpu.PrefetchScalarGridSpec(
            num_scalar_prefetch=1,
            grid=(1,),
            in_specs=[
                pl.BlockSpec(memory_space=pltpu.VMEM),
                pl.BlockSpec(memory_space=pltpu.VMEM),
                pl.BlockSpec((1, HALF), lambda i, ids: (0, ids[1])),
                pl.BlockSpec(memory_space=pltpu.SMEM),
            ],
            out_specs=[pl.BlockSpec(memory_space=pltpu.VMEM), pl.BlockSpec(memory_space=pltpu.VMEM)],
        ),
        compiler_params=pltpu.CompilerParams(vmem_limit_bytes=8 << 20),
        name="cast",
    )(ids, own, twin, gain.reshape(1, D), prior_peak)


def on_chip(x):
    return pltpu.with_memory_space_constraint(x, pltpu.VMEM)


def prefetch_body(source, target, sem):
    copy = pltpu.make_async_copy(source, target, sem)
    copy.start()
    copy.wait()


def prefetch(weight):
    return pl.pallas_call(
        prefetch_body,
        out_shape=jax.ShapeDtypeStruct(weight.shape, weight.dtype),
        in_specs=[pl.BlockSpec(memory_space=pltpu.HBM)],
        out_specs=pl.BlockSpec(memory_space=pltpu.VMEM),
        scratch_shapes=[pltpu.SemaphoreType.DMA],
        compiler_params=pltpu.CompilerParams(vmem_limit_bytes=8 << 20),
        name="prefetch",
    )(pltpu.with_memory_space_constraint(weight, pltpu.HBM))


K_TILE = 2048
NT_DIMS = (((1,), (1,)), ((), ()))


def half_product(weight, a, half):
    total = None
    for i in range(HALF // K_TILE):
        at = pl.multiple_of(half * HALF + i * K_TILE, K_TILE)
        tile = a[:, i * K_TILE : (i + 1) * K_TILE]
        part = lax.dot_general(weight[:, pl.ds(at, K_TILE)], tile, NT_DIMS, preferred_element_type=f32)
        total = part if total is None else total + part
    return total


def first_half_body(ids, weight, a, out):
    out[...] = half_product(weight, a, ids[1])


def first_half(ids, weight, a):
    return pl.pallas_call(
        first_half_body,
        out_shape=jax.ShapeDtypeStruct((weight.shape[0], TOK), f32),
        in_specs=[
            pl.BlockSpec(memory_space=pltpu.SMEM),
            pl.BlockSpec(memory_space=pltpu.VMEM),
            pl.BlockSpec(memory_space=pltpu.VMEM),
        ],
        out_specs=pl.BlockSpec(memory_space=pltpu.VMEM),
        compiler_params=pltpu.CompilerParams(vmem_limit_bytes=16 << 20),
        name="first_half",
    )(ids, on_chip(weight), a)


def both_parts(tail):
    wide = tail.astype(f32)
    return wide[:, 0:1] + wide[:, 1:2]


def second_half_body(ids, weight, a, start, arrived, twin, out, peak):
    total = start[...] + half_product(weight, a, ids[2])
    scaled = (total * arrived[0:1, HALF : HALF + 1].astype(f32)).astype(bf16)
    out[...] = jnp.dot(scaled, shuffle(ids[3]), preferred_element_type=f32).astype(bf16)
    peak[0] = jnp.max(jnp.maximum(both_parts(a[:, HALF:]), both_parts(twin[:, HALF:])))


def second_half(ids, weight, a, start, arrived, twin):
    return pl.pallas_call(
        second_half_body,
        out_shape=(jax.ShapeDtypeStruct((weight.shape[0], TOK), bf16), jax.ShapeDtypeStruct((1,), f32)),
        in_specs=[pl.BlockSpec(memory_space=pltpu.SMEM)] + [pl.BlockSpec(memory_space=pltpu.VMEM)] * 5,
        out_specs=[
            pl.BlockSpec(memory_space=pltpu.VMEM),
            pl.BlockSpec(memory_space=pltpu.SMEM),
        ],
        compiler_params=pltpu.CompilerParams(vmem_limit_bytes=16 << 20),
        name="second_half",
    )(ids, on_chip(weight), a, start, arrived, twin)


def cat(*blocks):
    return jnp.concatenate(blocks, axis=0)


def split(x):
    return [x[k * ROWS : (k + 1) * ROWS] for k in range(x.shape[0] // ROWS)]


def apart(first, *rest):
    return lax.optimization_barrier((first, *rest))


def packed(*blocks):
    return cat(*[b.astype(bf16) for b in blocks])


def reduce_rounds(kept, incoming):
    def block(o):
        rows = slice(o * ROWS, (o + 1) * ROWS)
        return kept[rows] + incoming[rows].astype(f32)

    out13, kept, incoming = apart(packed(block(13), block(11), block(7)), kept, incoming)
    a13 = across(out13, 1)
    out14, out15, kept, incoming = apart(packed(block(14)), packed(block(15)), kept, incoming)
    a14 = across(out14, 2)
    a15 = across(out15, 3)
    out9, kept, incoming = apart(packed(block(9), block(5), block(3), block(1)), kept, incoming)
    a9 = across(out9, 1)
    b13, b11, b7 = split(a13)
    out10, b13, kept, incoming = apart(
        packed(block(10) + b11.astype(f32), block(6) + b7.astype(f32)), b13, kept, incoming
    )
    a10 = across(out10, 2)
    out12, kept, incoming = apart(packed(block(12) + b13.astype(f32) + a14.astype(f32) + a15.astype(f32)), kept, incoming)
    a12 = across(out12, 4)
    c9, c5, c3, a1 = split(a9)
    c10, c6 = split(a10)
    out4, c9, c10, kept, incoming = apart(
        packed(block(4) + c5.astype(f32) + c6.astype(f32)), c9, c10, kept, incoming
    )
    a4 = across(out4, 4)
    total8 = packed(block(8) + c9.astype(f32) + c10.astype(f32) + a12.astype(f32))
    out8, c3, kept, incoming = apart(total8, c3, kept, incoming)
    a8 = across(out8, 8)
    a2 = across(packed(block(2) + c3.astype(f32)), 2)
    return block(0) + a1.astype(f32) + a2.astype(f32) + a4.astype(f32) + a8.astype(f32)


def gather_rounds(own):
    b = {0: own}
    for d in (8, 4, 2):
        b[d] = across(own, d)
    b[12] = across(b[8], 4)
    two = cat(b[8], b[4])
    b[10], b[6] = split(across(two, 2))
    b[9], b[5], b[3], b[1] = split(across(cat(b[8], b[4], b[2], own), 1))
    b[14] = across(b[12], 2)
    b[13], b[11], b[7] = split(across(cat(b[12], b[10], b[6]), 1))
    b[15] = across(b[12], 3)
    return cat(*[b[o] for o in range(CHIPS)])


def shards(sections, head_outputs, residual, out_weight, norm_gain, prior_peak, qkv_weight):
    heads = head_outputs[0]
    resid = residual[0]
    section = lax.axis_index("section")
    place = lax.axis_index("tp")
    z = place // 2
    core = place % 2
    label = z ^ jnp.where(section % 4 == 0, 8, 0)
    ids = jnp.stack([z, core, 1 - core, label]).astype(jnp.int32)

    weight = prefetch(qkv_weight.T)
    heads, resid, out_weight = [pltpu.with_memory_space_constraint(v, pltpu.HBM) for v in (heads, resid, out_weight)]
    outgoing = out_proj(ids, 2, heads, out_weight, resid, bf16)
    incoming = other_core(outgoing)
    kept = out_proj(ids, 1, heads, out_weight, resid, f32)
    own = lax.reduce_precision(reduce_rounds(kept, incoming), 8, 7).astype(bf16)
    twin = other_core(own)
    outbound, peaks = cast(ids, own, twin, norm_gain, prior_peak)
    arrived = next_section(outbound, sections)

    payload = jnp.concatenate([arrived[:, :HALF], peaks], axis=1)
    mine = gather_rounds(payload)
    theirs = other_core(mine)

    started = first_half(ids, weight, mine)
    columns, group_peak = second_half(ids, weight, theirs, started, arrived, mine)
    projected = columns.T

    first_row = core == 0
    own_rows = jnp.where(first_row, own[0:4], own[4:8])
    twin_rows = jnp.where(first_row, twin[0:4], twin[4:8])
    stream = jnp.where(
        first_row,
        jnp.concatenate([own_rows, twin_rows], axis=1),
        jnp.concatenate([twin_rows, own_rows], axis=1),
    )
    return (stream[None], projected[None], group_peak)


def solution(mesh):
    return jax.shard_map(
        functools.partial(shards, mesh.shape["section"]),
        mesh=mesh,
        in_specs=(
            P("section", None, "tp"),
            P("section", "tp", None),
            P("tp", None),
            P(),
            P("section"),
            P(None, "tp"),
        ),
        out_specs=(P("section", "tp", None), P("section", None, "tp"), P("section")),
        check_vma=False,
    )
```

```python
import functools
import jax
import jax.numpy as jnp
from jax import lax
from jax.experimental import pallas as pl
from jax.experimental.pallas import tpu as pltpu
from jax.sharding import PartitionSpec as P

epsilon = 1e-05
ceiling = 448.0

TP = 32
CHIPS = 16
ROWS = 8
TOK = 128
D = 8192
HALF = 4096
TAIL = 128
f32 = jnp.float32
bf16 = jnp.bfloat16


def across(x, d):
    return lax.ppermute(x, "tp", [(i, i ^ (2 * d)) for i in range(TP)])


def other_core(x):
    return lax.ppermute(x, "tp", [(i, i ^ 1) for i in range(TP)])


def next_section(x, sections):
    pairs = []
    for s in range(sections):
        shift = 16 if s % 4 == 3 else 0
        for t in range(TP):
            pairs.append((s * TP + t, ((s + 1) % sections) * TP + (t ^ shift)))
    return lax.ppermute(x, ("section", "tp"), pairs)


def shuffle(z):
    row = lax.broadcasted_iota(jnp.int32, (TOK, TOK), 0)
    col = lax.broadcasted_iota(jnp.int32, (TOK, TOK), 1)
    return jnp.where((row ^ (z * ROWS)) == col, 1.0, 0.0).astype(bf16)


N_TILE = 2048


def out_proj_body(ids, heads, weight, resid, out, rows):
    z = ids[0]
    core = ids[1]

    @pl.when(pl.program_id(0) == 0)
    def _():
        rows[...] = jnp.dot(shuffle(z), heads[...], preferred_element_type=f32).astype(bf16)

    product = jnp.dot(rows[...], weight[...], preferred_element_type=f32)
    out[...] = product.astype(out.dtype)
    mine = resid[...].astype(f32)
    zero = jnp.zeros_like(mine)
    eight = jnp.where(core == 0, jnp.concatenate([mine, zero], 0), jnp.concatenate([zero, mine], 0))
    out[0:ROWS, :] = (product[0:ROWS, :] + eight).astype(out.dtype)


def out_proj(ids, which, heads, weight, resid, dtype):
    tiles = HALF // N_TILE
    return pl.pallas_call(
        out_proj_body,
        out_shape=jax.ShapeDtypeStruct((TOK, HALF), dtype),
        grid_spec=pltpu.PrefetchScalarGridSpec(
            num_scalar_prefetch=1,
            grid=(tiles,),
            in_specs=[
                pl.BlockSpec((TOK, 256), lambda i, ids: (0, 0)),
                pl.BlockSpec((256, N_TILE), lambda i, ids: (0, ids[which] * tiles + i)),
                pl.BlockSpec((4, N_TILE), lambda i, ids: (0, ids[which] * tiles + i)),
            ],
            out_specs=pl.BlockSpec((TOK, N_TILE), lambda i, ids: (0, i)),
            scratch_shapes=[pltpu.VMEM((TOK, 256), bf16)],
        ),
        compiler_params=pltpu.CompilerParams(vmem_limit_bytes=16 << 20),
        name="out_proj",
    )(ids, heads, weight, resid)


def cast_body(ids, own, twin, gain, peak_in, payload, peaks):
    wide = own[...].astype(f32)
    wide_twin = twin[...].astype(f32)
    total = jnp.sum(wide * wide, axis=-1, keepdims=True) + jnp.sum(wide_twin * wide_twin, axis=-1, keepdims=True)
    normed = wide * lax.rsqrt(total / D + epsilon) * gain[...].astype(f32)
    unit = jnp.full((ROWS, TAIL), peak_in[0] / ceiling, f32).astype(bf16)
    payload[:, 0:HALF] = jnp.clip(normed / unit[:, 0:1].astype(f32), -ceiling, ceiling).astype(bf16)
    payload[:, HALF:] = unit
    peak = jnp.max(jnp.max(jnp.abs(normed), axis=1, keepdims=True), axis=0, keepdims=True)
    peak = jnp.broadcast_to(peak, (ROWS, TAIL))
    high = peak.astype(bf16)
    low = (peak - high.astype(f32)).astype(bf16)
    lane = lax.broadcasted_iota(jnp.int32, (ROWS, TAIL), 1)
    peaks[...] = jnp.where(lane == 0, high.astype(f32), low.astype(f32)).astype(bf16)


def cast(ids, own, twin, gain, prior_peak):
    return pl.pallas_call(
        cast_body,
        out_shape=(
            jax.ShapeDtypeStruct((ROWS, HALF + TAIL), bf16),
            jax.ShapeDtypeStruct((ROWS, TAIL), bf16),
        ),
        grid_spec=pltpu.PrefetchScalarGridSpec(
            num_scalar_prefetch=1,
            grid=(1,),
            in_specs=[
                pl.BlockSpec(memory_space=pltpu.VMEM),
                pl.BlockSpec(memory_space=pltpu.VMEM),
                pl.BlockSpec((1, HALF), lambda i, ids: (0, ids[1])),
                pl.BlockSpec(memory_space=pltpu.SMEM),
            ],
            out_specs=[pl.BlockSpec(memory_space=pltpu.VMEM), pl.BlockSpec(memory_space=pltpu.VMEM)],
        ),
        compiler_params=pltpu.CompilerParams(vmem_limit_bytes=8 << 20),
        name="cast",
    )(ids, own, twin, gain.reshape(1, D), prior_peak)


def on_chip(x):
    return pltpu.with_memory_space_constraint(x, pltpu.VMEM)


def prefetch_body(source, target, sem):
    copy = pltpu.make_async_copy(source, target, sem)
    copy.start()
    copy.wait()


def prefetch(weight):
    return pl.pallas_call(
        prefetch_body,
        out_shape=jax.ShapeDtypeStruct(weight.shape, weight.dtype),
        in_specs=[pl.BlockSpec(memory_space=pltpu.HBM)],
        out_specs=pl.BlockSpec(memory_space=pltpu.VMEM),
        scratch_shapes=[pltpu.SemaphoreType.DMA],
        compiler_params=pltpu.CompilerParams(vmem_limit_bytes=8 << 20),
        name="prefetch",
    )(pltpu.with_memory_space_constraint(weight, pltpu.HBM))


K_TILE = 2048
NT_DIMS = (((1,), (1,)), ((), ()))


def half_product(weight, a, half):
    total = None
    for i in range(HALF // K_TILE):
        at = pl.multiple_of(half * HALF + i * K_TILE, K_TILE)
        tile = a[:, i * K_TILE : (i + 1) * K_TILE]
        part = lax.dot_general(weight[:, pl.ds(at, K_TILE)], tile, NT_DIMS, preferred_element_type=f32)
        total = part if total is None else total + part
    return total


def first_half_body(ids, weight, a, out):
    out[...] = half_product(weight, a, ids[1])


def first_half(ids, weight, a):
    return pl.pallas_call(
        first_half_body,
        out_shape=jax.ShapeDtypeStruct((weight.shape[0], TOK), f32),
        in_specs=[
            pl.BlockSpec(memory_space=pltpu.SMEM),
            pl.BlockSpec(memory_space=pltpu.VMEM),
            pl.BlockSpec(memory_space=pltpu.VMEM),
        ],
        out_specs=pl.BlockSpec(memory_space=pltpu.VMEM),
        compiler_params=pltpu.CompilerParams(vmem_limit_bytes=16 << 20),
        name="first_half",
    )(ids, on_chip(weight), a)


def both_parts(tail):
    wide = tail.astype(f32)
    return wide[:, 0:1] + wide[:, 1:2]


def second_half_body(ids, weight, a, start, arrived, twin, out, peak):
    total = start[...] + half_product(weight, a, ids[2])
    scaled = (total * arrived[0:1, HALF : HALF + 1].astype(f32)).astype(bf16)
    out[...] = jnp.dot(scaled, shuffle(ids[3]), preferred_element_type=f32).astype(bf16)
    peak[0] = jnp.max(jnp.maximum(both_parts(a[:, HALF:]), both_parts(twin[:, HALF:])))


def second_half(ids, weight, a, start, arrived, twin):
    return pl.pallas_call(
        second_half_body,
        out_shape=(jax.ShapeDtypeStruct((weight.shape[0], TOK), bf16), jax.ShapeDtypeStruct((1,), f32)),
        in_specs=[pl.BlockSpec(memory_space=pltpu.SMEM)] + [pl.BlockSpec(memory_space=pltpu.VMEM)] * 5,
        out_specs=[
            pl.BlockSpec(memory_space=pltpu.VMEM),
            pl.BlockSpec(memory_space=pltpu.SMEM),
        ],
        compiler_params=pltpu.CompilerParams(vmem_limit_bytes=16 << 20),
        name="second_half",
    )(ids, on_chip(weight), a, start, arrived, twin)


def cat(*blocks):
    return jnp.concatenate(blocks, axis=0)


def split(x):
    return [x[k * ROWS : (k + 1) * ROWS] for k in range(x.shape[0] // ROWS)]


def apart(first, *rest):
    return lax.optimization_barrier((first, *rest))


def packed(*blocks):
    return cat(*[b.astype(bf16) for b in blocks])


def reduce_rounds(kept, incoming):
    def block(o):
        rows = slice(o * ROWS, (o + 1) * ROWS)
        return kept[rows] + incoming[rows].astype(f32)

    out15, kept, incoming = apart(block(15).astype(bf16), kept, incoming)
    a15 = across(out15, 1)
    out13, kept, incoming = apart(packed(block(13), block(11), block(7)), kept, incoming)
    a13 = across(out13, 1)
    out9, kept, incoming = apart(packed(block(9), block(5), block(3), block(1)), kept, incoming)
    a9 = across(out9, 1)
    out14, kept, incoming = apart(packed(block(14) + a15.astype(f32)), kept, incoming)
    a14 = across(out14, 2)
    b13, b11, b7 = split(a13)
    out10, b13, kept, incoming = apart(
        packed(block(10) + b11.astype(f32), block(6) + b7.astype(f32)), b13, kept, incoming
    )
    a10 = across(out10, 2)
    out12, kept, incoming = apart(packed(block(12) + b13.astype(f32) + a14.astype(f32)), kept, incoming)
    a12 = across(out12, 4)
    c9, c5, c3, a1 = split(a9)
    c10, c6 = split(a10)
    out4, c9, c10, kept, incoming = apart(
        packed(block(4) + c5.astype(f32) + c6.astype(f32)), c9, c10, kept, incoming
    )
    a4 = across(out4, 4)
    total8 = packed(block(8) + c9.astype(f32) + c10.astype(f32) + a12.astype(f32))
    out8, c3, kept, incoming = apart(total8, c3, kept, incoming)
    a8 = across(out8, 8)
    a2 = across(packed(block(2) + c3.astype(f32)), 2)
    return block(0) + a1.astype(f32) + a2.astype(f32) + a4.astype(f32) + a8.astype(f32)


def gather_rounds(own):
    b = {0: own}
    for d in (8, 4):
        b[d] = across(own, d)
    b[12] = across(b[8], 4)
    three = cat(b[8], b[4], own)
    b[10], b[6], b[2] = split(across(three, 2))
    b[9], b[5], b[1] = split(across(three, 1))
    b[14] = across(b[12], 2)
    b[13], b[11], b[7], b[3] = split(across(cat(b[12], b[10], b[6], b[2]), 1))
    b[15] = across(b[14], 1)
    return cat(*[b[o] for o in range(CHIPS)])


def shards(sections, head_outputs, residual, out_weight, norm_gain, prior_peak, qkv_weight):
    heads = head_outputs[0]
    resid = residual[0]
    section = lax.axis_index("section")
    place = lax.axis_index("tp")
    z = place // 2
    core = place % 2
    label = z ^ jnp.where(section % 4 == 0, 8, 0)
    ids = jnp.stack([z, core, 1 - core, label]).astype(jnp.int32)

    weight = prefetch(qkv_weight.T)
    heads, resid, out_weight = [pltpu.with_memory_space_constraint(v, pltpu.HBM) for v in (heads, resid, out_weight)]
    outgoing = out_proj(ids, 2, heads, out_weight, resid, bf16)
    incoming = other_core(outgoing)
    kept = out_proj(ids, 1, heads, out_weight, resid, f32)
    own = lax.reduce_precision(reduce_rounds(kept, incoming), 8, 7).astype(bf16)
    twin = other_core(own)
    outbound, peaks = cast(ids, own, twin, norm_gain, prior_peak)
    arrived = next_section(outbound, sections)

    payload = jnp.concatenate([arrived[:, :HALF], peaks], axis=1)
    mine = gather_rounds(payload)
    theirs = other_core(mine)

    started = first_half(ids, weight, mine)
    columns, group_peak = second_half(ids, weight, theirs, started, arrived, mine)
    projected = columns.T

    first_row = core == 0
    own_rows = jnp.where(first_row, own[0:4], own[4:8])
    twin_rows = jnp.where(first_row, twin[0:4], twin[4:8])
    stream = jnp.where(
        first_row,
        jnp.concatenate([own_rows, twin_rows], axis=1),
        jnp.concatenate([twin_rows, own_rows], axis=1),
    )
    return (stream[None], projected[None], group_peak)


def solution(mesh):
    return jax.shard_map(
        functools.partial(shards, mesh.shape["section"]),
        mesh=mesh,
        in_specs=(
            P("section", None, "tp"),
            P("section", "tp", None),
            P("tp", None),
            P(),
            P("section"),
            P(None, "tp"),
        ),
        out_specs=(P("section", "tp", None), P("section", None, "tp"), P("section")),
        check_vma=False,
    )
```
